512 devices in a mesh: gx: 128 (over x_lo, z, y), gy: 4 (over x_hi, core).
Axes of the slice: x: 4 (x_hi: 2, x_lo: 2; x = x_hi * 2 + x_lo), y: 4, z: 16, core: 2. Of those that a mesh axis runs over, the one named last changes fastest.
Arguments:
- populations: float32 [19, 1024, 64, 128], P(None, 'gx', 'gy'), as said below
- order_field: float32 [1024, 64, 128], P('gx', 'gy'), may hold values from -1 to 1
- solid_flags: int32 [1024, 64, 128], P('gx', 'gy'), may hold values 0 or 1
- plane_flags: int32 [128], replicated, may hold values 0 or 1
- shear_shift: int32 [1], replicated, may hold values from 1 to 63
- link_site: int32 [524288], P(('gx', 'gy')), may hold values from 0 to 16383, as said below
- link_dir: int32 [524288], P(('gx', 'gy')), may hold values from 1 to 18
- link_colloid: int32 [524288], P(('gx', 'gy')), may hold values from 0 to 2047
- link_count: int32 [4096], P(('gx', 'gy')), may hold values from 1 to 128, 327680 in all
- colloid_slot: int32 [2048], replicated, may hold values from 0 to 2047, each once
- colloid_speed: float32 [3, 2048], replicated, may hold values from -0.6 to 0.6
Outputs:
- new_populations: float32 [19, 1024, 64, 128], P(None, 'gx', 'gy')
- new_order: float32 [1024, 64, 128], P('gx', 'gy')
- colloid_force: float32 [3, 2048], P(None, ('gx', 'gy'))
The draws below stay inside these ranges and needn't reach their ends.
Inputs may be any that keep to these rules, and one draw needn't show every extreme that they name: `populations`: populations lie between 0.2 w_i and 1.8 w_i. `link_site`: the slots of one device name distinct sites in rising order, one in each run of (8 * 16 * 128) / 1024 sites.
All inputs are finite; a program needn't handle non-finite values. No bound on the sum of `solid_flags` or of `link_count` on one device may be relied on, other than what follows from the above.
Results may differ from the reference program's by a relative error of at most 0.00002.
Values sent between devices are 32-bit elements; how exact they have to be, the bound alone decides.
A program may use at most 64 MiB of HBM per device.

```python
import math
import jax
import jax.numpy as jnp
import numpy as np

Q = 19
CX = 8
CY = 16
NZ = 128
LINK_BLOCKS = 8
NX = 1024
NY = 64
SLABS = 128
LINKS_DEV = 1024
COLLOIDS = 2048
N_GY = 4
DEVICES = 512


def draw_populations(key, part):
    unit = jax.random.uniform(key, (Q, NX, NY, NZ), jnp.float32)
    factor = 0.2 + 1.6 * unit
    component = jnp.arange(Q).reshape((Q, 1, 1, 1))
    weight = jnp.where(component == 0, 1.0 / 3.0, jnp.where(component < 7, 1.0 / 18.0, 1.0 / 36.0))
    return (weight * factor).astype(jnp.float32)


def draw_link_site(key, part):
    stride = CX * CY * NZ // (LINK_BLOCKS * 128)
    count_all = DEVICES * LINK_BLOCKS * 128
    position = jnp.arange(count_all, dtype=jnp.int32) % (LINK_BLOCKS * 128)
    offset = jax.random.randint(key, (count_all,), 0, stride, dtype=jnp.int32)
    return (position * stride + offset).astype(jnp.int32)


def place_ends(drawn, rng, low, high):
    index_at = [jax.random.randint(jax.random.fold_in(rng, axis), (), 0, length) for axis, length in enumerate(drawn.shape)]
    longest = drawn.shape.index(max(drawn.shape))
    beside = index_at[:longest] + [(index_at[longest] + 1) % drawn.shape[longest]] + index_at[longest + 1:]
    return drawn.at[tuple(index_at)].set(low).at[tuple(beside)].set(high)


def shard_levels(stream_key, shape, split, low, largest):
    gain = 1.0
    for axis_at, parts in split:
        steps = jax.random.uniform(jax.random.fold_in(jax.random.fold_in(stream_key, 6), axis_at), (parts,), jnp.float32, low / len(split), largest / len(split))
        gain = gain * jnp.repeat(jnp.exp(steps), shape[axis_at] // parts).reshape((-1,) + (1,) * (len(shape) - 1 - axis_at))
    return gain


def length_profile(number_of, total, most, skew):
    portions = [(1 << 20) // math.isqrt(grade ** skew) + 1 for grade in range(2, number_of + 1)]
    surplus, holding = total - most - (number_of - 1), [1] * (number_of - 1)
    while surplus > 0:
        candidates = [i for i in range(number_of - 1) if holding[i] < most]
        mass, budget = sum([portions[i] for i in candidates]), surplus
        for i in candidates:
            more = min(most - holding[i], max(1, budget * portions[i] // mass), surplus)
            holding[i] = holding[i] + more
            surplus = surplus - more
    return np.array([most] + holding)


def uneven(own_key, number_of, total, bound, skew):
    if number_of == 2:
        one = jax.random.randint(own_key, (), max(1, total - bound), min(bound, total - 1) + 1)
        return jnp.stack([one, total - one])
    tallies = jnp.asarray(length_profile(number_of, total, bound, skew), jnp.int32)
    twos = (number_of - 1) // 2
    donor, receiver = tallies[1:1 + 2 * twos:2], tallies[2:2 + 2 * twos:2]
    margin = jnp.minimum(donor - 1, bound - receiver)
    passed = jax.random.randint(jax.random.fold_in(own_key, 1), (twos,), 0, 1 << 20) % (margin + 1)
    tallies = tallies.at[1:1 + 2 * twos:2].set(donor - passed).at[2:2 + 2 * twos:2].set(receiver + passed)
    return tallies[jax.random.permutation(jax.random.fold_in(own_key, 2), number_of)]


def gaussian(rng, dims, deviation, limit, held_as=jnp.bfloat16):
    values = deviation * jax.random.normal(rng, dims, jnp.float32)
    return jnp.clip(values, min=-limit, max=limit).astype(held_as)


def setup_inputs(seed: int = 0) -> dict:
    keys = jax.random.split(jax.random.key(seed), 12)
    return {
        "populations": draw_populations(jax.random.fold_in(keys[11], 71), 0),
        "order_field": jnp.clip(jax.random.uniform(keys[1], (NX, NY, NZ), jnp.float32, -1.0, 1.0) * shard_levels(keys[1], (NX, NY, NZ), ((0, 128), (1, 4)), -0.4, 0.0), -1.0, 1.0),
        "solid_flags": place_ends((jax.random.randint(keys[2], (NX, NY, NZ), 0, 8) < 1).astype(jnp.int32), jax.random.fold_in(keys[2], 1), 0, 1),
        "plane_flags": place_ends((jax.random.randint(keys[3], (SLABS,), 0, 2) < 1).astype(jnp.int32), jax.random.fold_in(keys[3], 1), 0, 1),
        "shear_shift": jax.random.randint(keys[4], (1,), 1, NY).astype(jnp.int32),
        "link_site": draw_link_site(jax.random.fold_in(keys[11], 71), 0),
        "link_dir": place_ends(jax.random.randint(keys[6], (DEVICES * LINKS_DEV,), 1, 19), jax.random.fold_in(keys[6], 1), 1, 18).astype(jnp.int32),
        "link_colloid": place_ends(jax.random.randint(keys[7], (DEVICES * LINKS_DEV,), 0, COLLOIDS), jax.random.fold_in(keys[7], 1), 0, COLLOIDS - 1).astype(jnp.int32),
        "link_count": uneven(keys[8], DEVICES * LINK_BLOCKS, DEVICES * LINK_BLOCKS * 80, 128, 2).astype(jnp.int32),
        "colloid_slot": jax.random.permutation(keys[9], COLLOIDS).astype(jnp.int32),
        "colloid_speed": gaussian(keys[10], (3, COLLOIDS), 0.1, 0.6, jnp.float32),
    }


VELOCITIES = [[0, 0, 0], [1, 0, 0], [-1, 0, 0], [0, 1, 0], [0, -1, 0], [0, 0, 1], [0, 0, -1], [1, 1, 0], [-1, -1, 0], [1, -1, 0], [-1, 1, 0], [1, 0, 1], [-1, 0, -1], [1, 0, -1], [-1, 0, 1], [0, 1, 1], [0, -1, -1], [0, 1, -1], [0, -1, 1]]
WEIGHTS = [1.0 / 3.0] + [1.0 / 18.0] * 6 + [1.0 / 36.0] * 12
OPPOSITE = [0, 2, 1, 4, 3, 6, 5, 8, 7, 10, 9, 12, 11, 14, 13, 16, 15, 18, 17]
TAU = 0.8
BULK = 0.04
KAPPA = 0.04
MOBILITY = 0.2
PLANE_SPEED = 0.05


def moments(stack):
    velocity_table = jnp.array(VELOCITIES, jnp.float32)
    shape = (19,) + (1,) * (stack.ndim - 1)
    density = jnp.sum(stack, axis=0)
    speed_x = jnp.sum(stack * velocity_table[:, 0].reshape(shape), axis=0) / density
    speed_y = jnp.sum(stack * velocity_table[:, 1].reshape(shape), axis=0) / density
    speed_z = jnp.sum(stack * velocity_table[:, 2].reshape(shape), axis=0) / density
    return density, speed_x, speed_y, speed_z


def boost_one(value, component, density, speed_x, speed_y, speed_z, change):
    east_step, north_step, upward_step = VELOCITIES[component]
    weight = WEIGHTS[component]
    projection = east_step * speed_x + north_step * speed_y + upward_step * speed_z
    shifted = projection + north_step * change
    square_old = speed_x * speed_x + speed_y * speed_y + speed_z * speed_z
    moved_y = speed_y + change
    square_new = speed_x * speed_x + moved_y * moved_y + speed_z * speed_z
    correction = weight * density * (3.0 * (shifted - projection) + 4.5 * (shifted * shifted - projection * projection) - 1.5 * (square_new - square_old))
    return value + correction


def collide(read, force_x, force_y, force_z):
    velocity_table = jnp.array(VELOCITIES, jnp.float32)
    shape = (19,) + (1,) * (read.ndim - 1)
    density = jnp.sum(read, axis=0)
    speed_x = (jnp.sum(read * velocity_table[:, 0].reshape(shape), axis=0) + 0.5 * force_x) / density
    speed_y = (jnp.sum(read * velocity_table[:, 1].reshape(shape), axis=0) + 0.5 * force_y) / density
    speed_z = (jnp.sum(read * velocity_table[:, 2].reshape(shape), axis=0) + 0.5 * force_z) / density
    square = speed_x * speed_x + speed_y * speed_y + speed_z * speed_z
    outputs = []
    for component in range(19):
        east_step, north_step, upward_step = VELOCITIES[component]
        weight = WEIGHTS[component]
        projection = east_step * speed_x + north_step * speed_y + upward_step * speed_z
        balance = weight * density * (1.0 + 3.0 * projection + 4.5 * projection * projection - 1.5 * square)
        along_force = east_step * force_x + north_step * force_y + upward_step * force_z
        forcing = weight * (3.0 * ((east_step - speed_x) * force_x + (north_step - speed_y) * force_y + (upward_step - speed_z) * force_z) + 9.0 * projection * along_force)
        outputs.append(read[component] - (read[component] - balance) / TAU + (1.0 - 0.5 / TAU) * forcing)
    return jnp.stack(outputs), speed_x, speed_y, speed_z


def reference(populations, order_field, solid_flags, plane_flags, shear_shift, link_site, link_dir, link_colloid, link_count, colloid_slot, colloid_speed):
    plane_shift = shear_shift[0]
    layers = jnp.arange(NX, dtype=jnp.int32)
    slab_of = layers // CX
    first_mask = (((layers % CX) == 0) & (plane_flags[slab_of] == 1))[:, None, None]
    last_mask = (((layers % CX) == CX - 1) & (plane_flags[(slab_of + 1) % SLABS] == 1))[:, None, None]
    density0, speed0_x, speed0_y, speed0_z = moments(populations)
    pieces = []
    for component in range(19):
        east_step, north_step, upward_step = VELOCITIES[component]
        plain = jnp.roll(populations[component], (east_step, north_step, upward_step), (0, 1, 2))
        if east_step == 1:
            boosted = boost_one(populations[component], component, density0, speed0_x, speed0_y, speed0_z, -PLANE_SPEED)
            pulled = jnp.roll(boosted, (1, north_step + plane_shift, upward_step), (0, 1, 2))
            plain = jnp.where(first_mask, pulled, plain)
        elif east_step == -1:
            boosted = boost_one(populations[component], component, density0, speed0_x, speed0_y, speed0_z, PLANE_SPEED)
            pulled = jnp.roll(boosted, (-1, north_step - plane_shift, upward_step), (0, 1, 2))
            plain = jnp.where(last_mask, pulled, plain)
        pieces.append(plain)
    read = jnp.stack(pieces)

    total_links = DEVICES * LINKS_DEV
    position = jnp.arange(total_links, dtype=jnp.int32)
    device = position // LINKS_DEV
    live_links = (position % 128) < link_count[position // 128]
    site_x = (device // N_GY) * CX + link_site // (CY * NZ)
    site_y = (device % N_GY) * CY + (link_site // NZ) % CY
    site_z = link_site % NZ
    velocity_table = jnp.array(VELOCITIES, jnp.float32)
    weight_table = jnp.array(WEIGHTS, jnp.float32)
    opposite_table = jnp.array(OPPOSITE, jnp.int32)
    source = populations[link_dir, site_x, site_y, site_z]
    direction_vec = velocity_table[link_dir]
    link_weight = weight_table[link_dir]
    link_speed = colloid_speed[:, link_colloid]
    projection = jnp.sum(direction_vec.T * link_speed, axis=0)
    returned = source - 6.0 * link_weight * projection
    target = opposite_table[link_dir]
    current = read[target, site_x, site_y, site_z]
    read = read.at[target, site_x, site_y, site_z].set(jnp.where(live_links, returned, current))
    transfer = jnp.where(live_links, 2.0 * source - 6.0 * link_weight * projection, 0.0) * direction_vec.T
    colloid_force = jax.ops.segment_sum(transfer.T, colloid_slot[link_colloid], num_segments=COLLOIDS).T

    def plus_x(values):
        return jnp.where(last_mask, jnp.roll(values, (-1, -plane_shift), (0, 1)), jnp.roll(values, -1, 0))

    def minus_x(values):
        return jnp.where(first_mask, jnp.roll(values, (1, plane_shift), (0, 1)), jnp.roll(values, 1, 0))

    def laplace(values):
        return plus_x(values) + minus_x(values) + jnp.roll(values, -1, 1) + jnp.roll(values, 1, 1) + jnp.roll(values, -1, 2) + jnp.roll(values, 1, 2) - 6.0 * values

    def gradient(values):
        return ((plus_x(values) - minus_x(values)) * 0.5, (jnp.roll(values, -1, 1) - jnp.roll(values, 1, 1)) * 0.5, (jnp.roll(values, -1, 2) - jnp.roll(values, 1, 2)) * 0.5)

    phase_now = order_field
    potential = BULK * (phase_now * phase_now * phase_now - phase_now) - KAPPA * laplace(phase_now)
    slope_x, slope_y, slope_z = gradient(potential)
    collided, speed_x, speed_y, speed_z = collide(read, -phase_now * slope_x, -phase_now * slope_y, -phase_now * slope_z)
    solid_mask = solid_flags == 1
    weight_shape = weight_table.reshape((19, 1, 1, 1))
    new_populations = jnp.where(solid_mask[None], weight_shape + 0.0 * collided, collided)
    phase_x, phase_y, phase_z = gradient(phase_now)
    advanced = phase_now - (speed_x * phase_x + speed_y * phase_y + speed_z * phase_z) + MOBILITY * laplace(potential)
    new_order = jnp.where(solid_mask, phase_now, advanced)
    return new_populations, new_order, colloid_force
```

```python
import jax
import jax.numpy as jnp
from jax import lax
from jax.experimental import pallas as pl
from jax.experimental.pallas import tpu as pltpu
from jax.sharding import PartitionSpec as P

VELOCITIES = [
    [0, 0, 0],
    [1, 0, 0],
    [-1, 0, 0],
    [0, 1, 0],
    [0, -1, 0],
    [0, 0, 1],
    [0, 0, -1],
    [1, 1, 0],
    [-1, -1, 0],
    [1, -1, 0],
    [-1, 1, 0],
    [1, 0, 1],
    [-1, 0, -1],
    [1, 0, -1],
    [-1, 0, 1],
    [0, 1, 1],
    [0, -1, -1],
    [0, 1, -1],
    [0, -1, 1],
]
WEIGHTS = [1.0 / 3.0] + [1.0 / 18.0] * 6 + [1.0 / 36.0] * 12
OPPOSITE = [0, 2, 1, 4, 3, 6, 5, 8, 7, 10, 9, 12, 11, 14, 13, 16, 15, 18, 17]
UP_X = [1, 7, 9, 11, 13]
DOWN_X = [2, 8, 10, 12, 14]
UP_Y = [3, 7, 10, 15, 17]
DOWN_Y = [4, 8, 9, 16, 18]
TAU = 0.8
BULK = 0.04
KAPPA = 0.04
MOBILITY = 0.2
PLANE_SPEED = 0.05

MESH = pl.DeviceIdType.MESH
CX, CY, NZ = 8, 16, 128
ROWS = CX * CY
PITCH = 32
NEAR, FAR = 32, 16
F32 = jnp.float32
I32 = jnp.int32


def iota(shape, dim):
    return lax.broadcasted_iota(I32, shape, dim)


def total(terms):
    terms = list(terms)
    while len(terms) > 1:
        terms = [
            terms[i] + terms[i + 1] if i + 1 < len(terms) else terms[i]
            for i in range(0, len(terms), 2)
        ]
    return terms[0]


def signed(values, axis):
    plus = total([values[c] for c in range(19) if VELOCITIES[c][axis] == 1])
    minus = total([values[c] for c in range(19) if VELOCITIES[c][axis] == -1])
    return plus - minus


def lanes_of(table, index):
    return jnp.take_along_axis(table, index, axis=1, mode="promise_in_bounds")


def build_face(pop, phi, out, components, row, phi_rows, change, flag):
    for half in range(2):
        at = pl.ds(row + 8 * half, 8)
        values = [pop[c, at, :] for c in range(19)]
        density = total(values)
        momentum = [signed(values, axis) for axis in range(3)]
        on = jnp.full((8, NZ), flag, I32) == 1
        for slot, c in enumerate(components):
            ex, ey, ez = VELOCITIES[c]
            along = total([e * m for e, m in zip((ex, ey, ez), momentum) if e])
            factor = 3.0 * ey * change + (4.5 * ey * ey - 1.5) * change * change
            correction = factor * density - (3.0 * change) * momentum[1]
            if ey:
                correction = correction + (9.0 * ey * change) * along
            boosted = values[c] + WEIGHTS[c] * correction
            out[slot, pl.ds(8 * half, 8), :] = jnp.where(on, boosted, values[c])
        for slot, phi_row in zip((5, 6), phi_rows):
            out[slot, pl.ds(8 * half, 8), :] = phi[pl.ds(phi_row + 8 * half, 8), :]


def build_rows(pop, phi, out, components, y, phi_ys):
    for slot, c in enumerate(components):
        out[slot] = pop[c, pl.ds(y, 8, stride=CY), :]
    for slot, py in zip((5, 6), phi_ys):
        out[slot] = phi[pl.ds(py, 8, stride=CY), :]


def build_links(pop, site, direction, colloid, count, speed, slots, dmap, wmap, smap, part):
    shape = (8, NZ)
    sub, lane = iota(shape, 0), iota(shape, 1)
    live_to = jnp.zeros(shape, I32)
    for a in range(8):
        live_to = jnp.where(sub == a, count[a], live_to)
    live = lane < live_to
    link_site, link_dir, link_colloid = site[...], direction[...], colloid[...]
    high, low = link_colloid >> 7, link_colloid & 127
    fetched = []
    for table, start in ((speed, 0), (speed, 16), (speed, 32), (slots, 0)):
        value = None
        for h in range(16):
            row = jnp.broadcast_to(table[pl.ds(start + h, 1), :], shape)
            got = lanes_of(row, low)
            value = got if value is None else jnp.where(high == h, got, value)
        fetched.append(value)
    ux, uy, uz, slot = fetched
    steps = []
    for axis in range(3):
        step = jnp.zeros(shape, F32)
        for c in range(1, 19):
            if VELOCITIES[c][axis]:
                step = jnp.where(link_dir == c, float(VELOCITIES[c][axis]), step)
        steps.append(step)
    weight = jnp.where(link_dir < 7, WEIGHTS[1], WEIGHTS[7])
    moved = 6.0 * weight * (steps[0] * ux + steps[1] * uy + steps[2] * uz)
    packed = (link_site & 15) + 16 * jnp.where(live, link_dir, 0)
    for a in range(8):
        packed_row = jnp.broadcast_to(packed[a : a + 1], shape)
        moved_row = jnp.broadcast_to(moved[a : a + 1], shape)
        for half in range(2):
            rows = pl.ds(a * CY + 8 * half, 8)
            index = 8 * (sub + 8 * half) + (lane >> 4)
            code = lanes_of(packed_row, index)
            d = jnp.where((code & 15) == (lane & 15), code >> 4, 0)
            source = jnp.zeros(shape, F32)
            for c in range(1, 19):
                source = jnp.where(d == c, pop[c, rows, :], source)
            dmap[rows, :] = d
            smap[rows, :] = source
            wmap[rows, :] = source - lanes_of(moved_row, index)
    link_z = link_site & 127
    source = jnp.zeros(shape, F32)
    for y in range(CY):
        got = lanes_of(smap[pl.ds(y, 8, stride=CY), :], link_z)
        source = jnp.where((lane >> 3) == y, got, source)
    momentum = jnp.where(live, 2.0 * source - moved, 0.0)
    target = (slot >> 2) & 31
    column = (slot >> 7) * 4 + (slot & 3)
    pieces = [[], [], []]
    for axis in range(3):
        left = steps[axis] * momentum
        for split in range(3):
            piece = left.astype(jnp.bfloat16).astype(F32)
            left = left - piece
            pieces[split].append(piece)
    kind = sub & 3
    left_rows, right_rows = [[], [], []], []
    big = iota((NZ, NZ), 0)
    for a in range(8):
        spread = [
            [jnp.broadcast_to(pieces[s][axis][a : a + 1], shape) for axis in range(3)]
            for s in range(3)
        ]
        pattern = [
            jnp.where(kind == 0, p[0], jnp.where(kind == 1, p[1], jnp.where(kind == 2, p[2], 0.0)))
            for p in spread
        ]
        goes = jnp.broadcast_to(target[a : a + 1], (NZ, NZ)) == (big >> 2)
        for s in range(3):
            full = jnp.broadcast_to(pattern[s][None], (16, 8, NZ)).reshape(NZ, NZ)
            left_rows[s].append(jnp.where(goes, full, 0.0).astype(jnp.bfloat16))
        right_rows.append(
            jnp.where(jnp.broadcast_to(column[a : a + 1], (NZ, NZ)) == big, 1.0, 0.0).astype(
                jnp.bfloat16
            )
        )
    left_matrix = jnp.concatenate([jnp.concatenate(r, axis=1) for r in left_rows], axis=0)
    right_matrix = jnp.concatenate(right_rows, axis=1)
    product = lax.dot_general(
        left_matrix, right_matrix, (((1,), (1,)), ((), ())), preferred_element_type=F32
    )
    product = product[0:NZ] + product[NZ : 2 * NZ] + product[2 * NZ :]
    part[...] = product.reshape(NEAR, 4, NZ)


def prepare(
    pop,
    phi,
    flags,
    site,
    direction,
    colloid,
    count,
    speed,
    slots,
    up_face,
    down_face,
    high_rows,
    low_rows,
    part,
    dmap,
    wmap,
    smap,
):
    gx = lax.axis_index("gx")
    plane_low = flags[gx]
    plane_high = flags[lax.rem(gx + 1, 128)]
    build_face(pop, phi, up_face, UP_X, 112, (96, 112), -PLANE_SPEED, plane_high)
    build_face(pop, phi, down_face, DOWN_X, 0, (0, 16), PLANE_SPEED, plane_low)
    build_rows(pop, phi, high_rows, UP_Y, CY - 1, (CY - 2, CY - 1))
    build_rows(pop, phi, low_rows, DOWN_Y, 0, (0, 1))
    build_links(pop, site, direction, colloid, count, speed, slots, dmap, wmap, smap, part)


def exchange(
    up_face,
    down_face,
    high_rows,
    low_rows,
    part,
    below,
    above,
    south,
    north,
    force,
    near,
    far,
    near_send,
    near_recv,
    far_send,
    far_recv,
    face_send,
    face_recv,
    row_send,
    row_recv,
):
    gx, gy = lax.axis_index("gx"), lax.axis_index("gy")
    slab_up, slab_down = lax.rem(gx + 1, 128), lax.rem(gx + 127, 128)
    near_base = (gx // 8) * 8
    near_me = (gx % 8) * 4 + gy
    far_me = gx // 8
    far_base = gx % 8

    def near_id(k):
        t = lax.rem(near_me + k, NEAR)
        return t, (near_base + t // 4, lax.rem(t, 4))

    def far_id(k):
        h = lax.rem(far_me + k, FAR)
        return h, (h * 8 + far_base, gy)

    barrier = pltpu.get_barrier_semaphore()

    def greet(device):
        pl.semaphore_signal(barrier, inc=1, device_id=device, device_id_type=MESH)

    @pl.loop(1, FAR)
    def _(k):
        greet(far_id(k)[1])

    for slab in (slab_up, slab_down):
        for g in range(4):
            greet((slab, g))

    @pl.loop(1, NEAR)
    def _(k):
        greet(near_id(k)[1])

    pl.semaphore_wait(barrier, FAR - 1 + 8 + NEAR - 1)

    def near_copy(k):
        t, device = near_id(k)
        return pltpu.make_async_remote_copy(
            src_ref=part.at[t],
            dst_ref=near.at[near_me],
            send_sem=near_send.at[t],
            recv_sem=near_recv.at[near_me],
            device_id=device,
            device_id_type=MESH,
        )

    def far_copy(k):
        h, device = far_id(k)
        return pltpu.make_async_remote_copy(
            src_ref=far.at[far_me],
            dst_ref=far.at[far_me],
            send_sem=far_send.at[h],
            recv_sem=far_recv.at[far_me],
            device_id=device,
            device_id_type=MESH,
        )

    rows = pl.ds(pl.multiple_of(gy * CY, CY), CY)
    faces = []
    for side, (src, dst, slab) in enumerate(
        ((up_face, below, slab_up), (down_face, above, slab_down))
    ):
        for g in range(4):
            faces.append(
                pltpu.make_async_remote_copy(
                    src_ref=src,
                    dst_ref=dst.at[:, rows, :],
                    send_sem=face_send.at[side, g],
                    recv_sem=face_recv.at[side, gy],
                    device_id=(slab, g),
                    device_id_type=MESH,
                )
            )
    edges = []
    for side, (src, dst, g) in enumerate(
        ((high_rows, south, lax.rem(gy + 1, 4)), (low_rows, north, lax.rem(gy + 3, 4)))
    ):
        edges.append(
            pltpu.make_async_remote_copy(
                src_ref=src,
                dst_ref=dst,
                send_sem=row_send.at[side],
                recv_sem=row_recv.at[side],
                device_id=(gx, g),
                device_id_type=MESH,
            )
        )

    @pl.loop(1, NEAR)
    def _(k):
        near_copy(k).start()

    for copy in faces:
        copy.start()
    for copy in edges:
        copy.start()

    near[near_me] = part[near_me]

    def arrived(buffer, sem, slot):
        pltpu.make_async_copy(buffer.at[slot], buffer.at[slot], sem.at[slot]).wait()

    @pl.loop(1, NEAR)
    def _(k):
        arrived(near, near_recv, lax.rem(near_me + k, NEAR))

    far[far_me] = total([near[t] for t in range(NEAR)])

    @pl.loop(1, FAR)
    def _(k):
        far_copy(k).start()

    for side, dst in enumerate((below, above)):
        for g in range(4):
            block = dst.at[:, pl.ds(g * CY, CY), :]
            pltpu.make_async_copy(block, block, face_recv.at[side, g]).wait()
    for copy in edges:
        copy.wait_recv()

    @pl.loop(1, FAR)
    def _(k):
        arrived(far, far_recv, lax.rem(far_me + k, FAR))

    summed = total([far[h] for h in range(FAR)])
    force[...] = summed

    for copy in faces + edges:
        copy.wait_send()

    @pl.loop(1, NEAR)
    def _(k):
        near_copy(k).wait_send()

    @pl.loop(1, FAR)
    def _(k):
        far_copy(k).wait_send()


def assemble(pop, phi, below, above, south, north, flags, shift, ext, order):
    gx, gy = lax.axis_index("gx"), lax.axis_index("gy")
    s = shift[0]
    low = s * flags[gx]
    high = s * flags[lax.rem(gx + 1, 128)]
    for x in range(CX):
        own = pl.ds(x * CY, CY)
        order[pl.ds((x + 2) * PITCH + 8, CY), :] = phi[own, :]
        for c in range(19):
            ext[c, pl.ds((x + 1) * PITCH + 8, CY), :] = pop[c, own, :]
    for f in range(7):
        for dst in (below, above):
            for r in range(0, 24, 8):
                dst[f, pl.ds(64 + r, 8), :] = dst[f, pl.ds(r, 8), :]
    begin_low = lax.rem(gy * CY - 2 - low + 128, 64)
    begin_high = lax.rem(gy * CY - 2 + high + 128, 64)
    for src, begin, components, layer, layers in (
        (below, begin_low, UP_X, 0, (0, 1)),
        (above, begin_high, DOWN_X, 9, (10, 11)),
    ):
        for f, c in enumerate(components):
            for k in (0, 8, 10):
                ext[c, pl.ds(layer * PITCH + 7 + k, 8), :] = src[f, pl.ds(begin + 1 + k, 8), :]
        for f, l in zip((5, 6), layers):
            for k in (0, 8, 12):
                order[pl.ds(l * PITCH + 6 + k, 8), :] = src[f, pl.ds(begin + k, 8), :]
    for f in range(5):
        ext[UP_Y[f], pl.ds(PITCH + 7, 8, stride=PITCH), :] = south[f]
        ext[DOWN_Y[f], pl.ds(PITCH + 24, 8, stride=PITCH), :] = north[f]
    order[pl.ds(2 * PITCH + 6, 8, stride=PITCH), :] = south[5]
    order[pl.ds(2 * PITCH + 7, 8, stride=PITCH), :] = south[6]
    order[pl.ds(2 * PITCH + 24, 8, stride=PITCH), :] = north[5]
    order[pl.ds(2 * PITCH + 25, 8, stride=PITCH), :] = north[6]


def turn(value, step):
    return pltpu.roll(value, step % NZ, 1)


def laplace(ref, at):
    centre = ref[pl.ds(at, 8), :]
    return (
        ref[pl.ds(at + PITCH, 8), :]
        + ref[pl.ds(at - PITCH, 8), :]
        + ref[pl.ds(at + 1, 8), :]
        + ref[pl.ds(at - 1, 8), :]
        + turn(centre, -1)
        + turn(centre, 1)
        - 6.0 * centre
    )


def gradient(ref, at):
    centre = ref[pl.ds(at, 8), :]
    return (
        (ref[pl.ds(at + PITCH, 8), :] - ref[pl.ds(at - PITCH, 8), :]) * 0.5,
        (ref[pl.ds(at + 1, 8), :] - ref[pl.ds(at - 1, 8), :]) * 0.5,
        (turn(centre, -1) - turn(centre, 1)) * 0.5,
    )


def collide(ext, order, potential, solid, dmap, wmap, new_pop, new_order):
    @pl.loop(0, CX + 2)
    def _(layer):
        at = pl.multiple_of(layer * PITCH, PITCH)
        for k in (7, 15, 17):
            v = order[pl.ds(at + PITCH + k, 8), :]
            curve = laplace(order, at + PITCH + k)
            potential[pl.ds(at + k, 8), :] = BULK * (v * v * v - v) - KAPPA * curve

    @pl.loop(0, CX)
    def _(x):
        for half in range(2):
            at = pl.multiple_of((x + 1) * PITCH, PITCH) + 8 + 8 * half
            out_rows = pl.ds(pl.multiple_of(x * CY, CY) + 8 * half, 8)
            d = dmap[out_rows, :]
            w = wmap[out_rows, :]
            read = []
            for c in range(19):
                ex, ey, ez = VELOCITIES[c]
                value = ext[c, pl.ds(at - ex * PITCH - ey, 8), :]
                if ez:
                    value = turn(value, ez)
                if c:
                    value = jnp.where(d == OPPOSITE[c], w, value)
                read.append(value)
            phi = order[pl.ds(at + PITCH, 8), :]
            slopes = gradient(potential, at)
            force = [-phi * slope for slope in slopes]
            density = total(read)
            inverse = 1.0 / density
            speed = [(signed(read, axis) + 0.5 * force[axis]) * inverse for axis in range(3)]
            square = speed[0] * speed[0] + speed[1] * speed[1] + speed[2] * speed[2]
            work = speed[0] * force[0] + speed[1] * force[1] + speed[2] * force[2]
            still = solid[out_rows, :] == 1
            half_force = 1.0 - 0.5 / TAU
            base = density * (1.0 / TAU) * (1.0 - 1.5 * square) - (3.0 * half_force) * work
            scaled = density * (1.0 / TAU)
            for c in range(19):
                ex, ey, ez = VELOCITIES[c]
                keep = read[c] * (1.0 - 1.0 / TAU)
                if c == 0:
                    value = keep + WEIGHTS[0] * base
                else:
                    cu = total([e * v for e, v in zip((ex, ey, ez), speed) if e])
                    cf = total([e * v for e, v in zip((ex, ey, ez), force) if e])
                    value = keep + WEIGHTS[c] * (
                        base
                        + scaled * (cu * (3.0 + 4.5 * cu))
                        + (half_force * cf) * (3.0 + 9.0 * cu)
                    )
                new_pop[c, out_rows, :] = jnp.where(still, WEIGHTS[c], value)
            px, py, pz = gradient(order, at + PITCH)
            curve = laplace(potential, at)
            advanced = phi - (speed[0] * px + speed[1] * py + speed[2] * pz) + MOBILITY * curve
            new_order[out_rows, :] = jnp.where(still, phi, advanced)


def finish(
    pop,
    phi,
    solid,
    flags,
    shift,
    below_in,
    above_in,
    south,
    north,
    dmap,
    wmap,
    new_pop,
    new_order,
    below,
    above,
    ext,
    order,
    potential,
):
    below[:, 0:64, :] = below_in[...]
    above[:, 0:64, :] = above_in[...]
    assemble(pop, phi, below, above, south, north, flags, shift, ext, order)
    collide(ext, order, potential, solid, dmap, wmap, new_pop, new_order)


VM = pl.BlockSpec(memory_space=pltpu.VMEM)
SM = pl.BlockSpec(memory_space=pltpu.SMEM)


def shaped(*dims, dtype=F32):
    return jax.ShapeDtypeStruct(dims, dtype)


def per_device(
    populations,
    order_field,
    solid_flags,
    plane_flags,
    shear_shift,
    link_site,
    link_dir,
    link_colloid,
    link_count,
    colloid_slot,
    colloid_speed,
):
    pop = populations.reshape(19, ROWS, NZ)
    phi = order_field.reshape(ROWS, NZ)
    solid = solid_flags.reshape(ROWS, NZ)
    up_face, down_face, high_rows, low_rows, part, dmap, wmap = pl.pallas_call(
        prepare,
        out_shape=(
            shaped(7, CY, NZ),
            shaped(7, CY, NZ),
            shaped(7, 8, NZ),
            shaped(7, 8, NZ),
            shaped(NEAR, 4, NZ),
            shaped(ROWS, NZ, dtype=I32),
            shaped(ROWS, NZ),
        ),
        in_specs=[VM, VM, SM, VM, VM, VM, SM, VM, VM],
        out_specs=[VM] * 7,
        scratch_shapes=[pltpu.VMEM((ROWS, NZ), F32)],
        name="prepare",
    )(
        pop,
        phi,
        plane_flags,
        link_site.reshape(8, NZ),
        link_dir.reshape(8, NZ),
        link_colloid.reshape(8, NZ),
        link_count,
        colloid_speed.reshape(48, NZ),
        colloid_slot.reshape(16, NZ),
    )
    below, above, south, north, force = pl.pallas_call(
        exchange,
        out_shape=(
            shaped(7, 64, NZ),
            shaped(7, 64, NZ),
            shaped(7, 8, NZ),
            shaped(7, 8, NZ),
            shaped(4, NZ),
        ),
        in_specs=[VM] * 5,
        out_specs=[VM] * 5,
        scratch_shapes=[
            pltpu.VMEM((NEAR, 4, NZ), F32),
            pltpu.VMEM((FAR, 4, NZ), F32),
            pltpu.SemaphoreType.DMA((NEAR,)),
            pltpu.SemaphoreType.DMA((NEAR,)),
            pltpu.SemaphoreType.DMA((FAR,)),
            pltpu.SemaphoreType.DMA((FAR,)),
            pltpu.SemaphoreType.DMA((2, 4)),
            pltpu.SemaphoreType.DMA((2, 4)),
            pltpu.SemaphoreType.DMA((2,)),
            pltpu.SemaphoreType.DMA((2,)),
        ],
        compiler_params=pltpu.CompilerParams(collective_id=0, has_side_effects=True),
        name="exchange",
    )(up_face, down_face, high_rows, low_rows, part)
    new_pop, new_order = pl.pallas_call(
        finish,
        out_shape=(shaped(19, ROWS, NZ), shaped(ROWS, NZ)),
        in_specs=[VM, VM, VM, SM, SM] + [VM] * 6,
        out_specs=[VM] * 2,
        scratch_shapes=[
            pltpu.VMEM((7, 88, NZ), F32),
            pltpu.VMEM((7, 88, NZ), F32),
            pltpu.VMEM((19, 10 * PITCH, NZ), F32),
            pltpu.VMEM((12 * PITCH, NZ), F32),
            pltpu.VMEM((10 * PITCH, NZ), F32),
        ],
        name="finish",
    )(
        pop,
        phi,
        solid,
        plane_flags,
        shear_shift,
        below,
        above,
        south,
        north,
        dmap,
        wmap,
    )
    owner = lax.axis_index("gx") // 8
    colloid_force = lax.dynamic_slice(force, (0, owner * 4), (3, 4))
    return (
        new_pop.reshape(populations.shape),
        new_order.reshape(order_field.shape),
        colloid_force,
    )


def solution(mesh):
    return jax.shard_map(
        per_device,
        mesh=mesh,
        in_specs=(
            P(None, "gx", "gy", None),
            P("gx", "gy", None),
            P("gx", "gy", None),
            P(),
            P(),
            P(("gx", "gy")),
            P(("gx", "gy")),
            P(("gx", "gy")),
            P(("gx", "gy")),
            P(),
            P(),
        ),
        out_specs=(P(None, "gx", "gy", None), P("gx", "gy", None), P(None, ("gx", "gy"))),
        check_vma=False,
    )
```

```python
import jax
import jax.numpy as jnp
from jax import lax
from jax.experimental import pallas as pl
from jax.experimental.pallas import tpu as pltpu
from jax.sharding import PartitionSpec as P

VELOCITIES = [
    [0, 0, 0],
    [1, 0, 0],
    [-1, 0, 0],
    [0, 1, 0],
    [0, -1, 0],
    [0, 0, 1],
    [0, 0, -1],
    [1, 1, 0],
    [-1, -1, 0],
    [1, -1, 0],
    [-1, 1, 0],
    [1, 0, 1],
    [-1, 0, -1],
    [1, 0, -1],
    [-1, 0, 1],
    [0, 1, 1],
    [0, -1, -1],
    [0, 1, -1],
    [0, -1, 1],
]
WEIGHTS = [1.0 / 3.0] + [1.0 / 18.0] * 6 + [1.0 / 36.0] * 12
OPPOSITE = [0, 2, 1, 4, 3, 6, 5, 8, 7, 10, 9, 12, 11, 14, 13, 16, 15, 18, 17]
UP_X = [1, 7, 9, 11, 13]
DOWN_X = [2, 8, 10, 12, 14]
UP_Y = [3, 7, 10, 15, 17]
DOWN_Y = [4, 8, 9, 16, 18]
TAU = 0.8
BULK = 0.04
KAPPA = 0.04
MOBILITY = 0.2
PLANE_SPEED = 0.05

MESH = pl.DeviceIdType.MESH
CX, CY, NZ = 8, 16, 128
ROWS = CX * CY
PITCH = 32
NEAR, FAR = 32, 16
F32 = jnp.float32
I32 = jnp.int32


def iota(shape, dim):
    return lax.broadcasted_iota(I32, shape, dim)


def total(terms):
    terms = list(terms)
    while len(terms) > 1:
        terms = [
            terms[i] + terms[i + 1] if i + 1 < len(terms) else terms[i]
            for i in range(0, len(terms), 2)
        ]
    return terms[0]


def signed(values, axis):
    plus = total([values[c] for c in range(19) if VELOCITIES[c][axis] == 1])
    minus = total([values[c] for c in range(19) if VELOCITIES[c][axis] == -1])
    return plus - minus


def lanes_of(table, index):
    return jnp.take_along_axis(table, index, axis=1, mode="promise_in_bounds")


def build_face(pop, phi, out, components, row, phi_rows, change, flag):
    for half in range(2):
        at = pl.ds(row + 8 * half, 8)
        values = [pop[c, at, :] for c in range(19)]
        density = total(values)
        momentum = [signed(values, axis) for axis in range(3)]
        on = jnp.full((8, NZ), flag, I32) == 1
        for slot, c in enumerate(components):
            ex, ey, ez = VELOCITIES[c]
            along = total([e * m for e, m in zip((ex, ey, ez), momentum) if e])
            factor = 3.0 * ey * change + (4.5 * ey * ey - 1.5) * change * change
            correction = factor * density - (3.0 * change) * momentum[1]
            if ey:
                correction = correction + (9.0 * ey * change) * along
            boosted = values[c] + WEIGHTS[c] * correction
            out[slot, pl.ds(8 * half, 8), :] = jnp.where(on, boosted, values[c])
        for slot, phi_row in zip((5, 6), phi_rows):
            out[slot, pl.ds(8 * half, 8), :] = phi[pl.ds(phi_row + 8 * half, 8), :]


def build_rows(pop, phi, out, components, y, phi_ys):
    for slot, c in enumerate(components):
        out[slot] = pop[c, pl.ds(PITCH + 8 + y, 8, stride=PITCH), :]
    for slot, py in zip((5, 6), phi_ys):
        out[slot] = phi[pl.ds(py, 8, stride=CY), :]


def build_links(pop, site, direction, colloid, count, speed, slots, dmap, wmap, smap, part):
    shape = (8, NZ)
    sub, lane = iota(shape, 0), iota(shape, 1)
    live_to = jnp.zeros(shape, I32)
    for a in range(8):
        live_to = jnp.where(sub == a, count[a], live_to)
    live = lane < live_to
    link_site, link_dir, link_colloid = site[...], direction[...], colloid[...]
    high, low = link_colloid >> 7, link_colloid & 127
    fetched = []
    for axis in range(4):
        value = None
        for h in range(16):
            if axis < 3:
                row = speed[pl.ds(axis, 1), pl.ds(h * NZ, NZ)]
            else:
                row = slots[pl.ds(h, 1), :]
            row = jnp.broadcast_to(row, shape)
            got = lanes_of(row, low)
            value = got if value is None else jnp.where(high == h, got, value)
        fetched.append(value)
    ux, uy, uz, slot = fetched
    steps = []
    for axis in range(3):
        step = jnp.zeros(shape, F32)
        for c in range(1, 19):
            if VELOCITIES[c][axis]:
                step = jnp.where(link_dir == c, float(VELOCITIES[c][axis]), step)
        steps.append(step)
    weight = jnp.where(link_dir < 7, WEIGHTS[1], WEIGHTS[7])
    moved = 6.0 * weight * (steps[0] * ux + steps[1] * uy + steps[2] * uz)
    packed = (link_site & 15) + 16 * jnp.where(live, link_dir, 0)
    for a in range(8):
        packed_row = jnp.broadcast_to(packed[a : a + 1], shape)
        moved_row = jnp.broadcast_to(moved[a : a + 1], shape)
        for half in range(2):
            rows = pl.ds(a * CY + 8 * half, 8)
            index = 8 * (sub + 8 * half) + (lane >> 4)
            code = lanes_of(packed_row, index)
            d = jnp.where((code & 15) == (lane & 15), code >> 4, 0)
            source = jnp.zeros(shape, F32)
            for c in range(1, 19):
                source = jnp.where(d == c, pop[c, pl.ds((a + 1) * PITCH + 8 + 8 * half, 8), :], source)
            dmap[rows, :] = d
            smap[rows, :] = source
            wmap[rows, :] = source - lanes_of(moved_row, index)
    link_z = link_site & 127
    source = jnp.zeros(shape, F32)
    for y in range(CY):
        got = lanes_of(smap[pl.ds(y, 8, stride=CY), :], link_z)
        source = jnp.where((lane >> 3) == y, got, source)
    momentum = jnp.where(live, 2.0 * source - moved, 0.0)
    target = (slot >> 10) * 16 + ((slot >> 2) & 15)
    column = ((slot >> 6) & 15) * 4 + (slot & 3)
    pieces = [[], [], []]
    for axis in range(3):
        left = steps[axis] * momentum
        for split in range(3):
            piece = left.astype(jnp.bfloat16).astype(F32)
            left = left - piece
            pieces[split].append(piece)
    kind = sub & 3
    left_rows, right_rows = [[], [], []], []
    big = iota((NZ, NZ), 0)
    for a in range(8):
        spread = [
            [jnp.broadcast_to(pieces[s][axis][a : a + 1], shape) for axis in range(3)]
            for s in range(3)
        ]
        pattern = [
            jnp.where(kind == 0, p[0], jnp.where(kind == 1, p[1], jnp.where(kind == 2, p[2], 0.0)))
            for p in spread
        ]
        goes = jnp.broadcast_to(target[a : a + 1], (NZ, NZ)) == (big >> 2)
        for s in range(3):
            full = jnp.broadcast_to(pattern[s][None], (16, 8, NZ)).reshape(NZ, NZ)
            left_rows[s].append(jnp.where(goes, full, 0.0).astype(jnp.bfloat16))
        right_rows.append(
            jnp.where(jnp.broadcast_to(column[a : a + 1], (NZ, NZ)) == big, 1.0, 0.0).astype(
                jnp.bfloat16
            )
        )
    left_matrix = jnp.concatenate([jnp.concatenate(r, axis=1) for r in left_rows], axis=0)
    right_matrix = jnp.concatenate(right_rows, axis=1)
    product = lax.dot_general(
        left_matrix, right_matrix, (((1,), (1,)), ((), ())), preferred_element_type=F32
    )
    product = product[0:NZ] + product[NZ : 2 * NZ] + product[2 * NZ :]
    part[...] = product.reshape(NEAR, 4, NZ)


def turn(value, step):
    return pltpu.roll(value, step % NZ, 1)


def laplace(ref, at):
    centre = ref[pl.ds(at, 8), :]
    return (
        ref[pl.ds(at + PITCH, 8), :]
        + ref[pl.ds(at - PITCH, 8), :]
        + ref[pl.ds(at + 1, 8), :]
        + ref[pl.ds(at - 1, 8), :]
        + turn(centre, -1)
        + turn(centre, 1)
        - 6.0 * centre
    )


def gradient(ref, at):
    centre = ref[pl.ds(at, 8), :]
    return (
        (ref[pl.ds(at + PITCH, 8), :] - ref[pl.ds(at - PITCH, 8), :]) * 0.5,
        (ref[pl.ds(at + 1, 8), :] - ref[pl.ds(at - 1, 8), :]) * 0.5,
        (turn(centre, -1) - turn(centre, 1)) * 0.5,
    )


def collide(ext, order, potential, solid, dmap, wmap, new_pop, new_order):
    @pl.loop(0, CX + 2)
    def _(layer):
        at = pl.multiple_of(layer * PITCH, PITCH)
        for k in (7, 15, 17):
            v = order[pl.ds(at + PITCH + k, 8), :]
            curve = laplace(order, at + PITCH + k)
            potential[pl.ds(at + k, 8), :] = BULK * (v * v * v - v) - KAPPA * curve

    @pl.loop(0, CX)
    def _(x):
        for half in range(2):
            at = pl.multiple_of((x + 1) * PITCH, PITCH) + 8 + 8 * half
            out_rows = pl.ds(pl.multiple_of(x * CY, CY) + 8 * half, 8)
            d = dmap[out_rows, :]
            w = wmap[out_rows, :]
            read = []
            for c in range(19):
                ex, ey, ez = VELOCITIES[c]
                value = ext[c, pl.ds(at - ex * PITCH - ey, 8), :]
                if ez:
                    value = turn(value, ez)
                if c:
                    value = jnp.where(d == OPPOSITE[c], w, value)
                read.append(value)
            phi = order[pl.ds(at + PITCH, 8), :]
            slopes = gradient(potential, at)
            force = [-phi * slope for slope in slopes]
            density = total(read)
            inverse = 1.0 / density
            speed = [(signed(read, axis) + 0.5 * force[axis]) * inverse for axis in range(3)]
            square = speed[0] * speed[0] + speed[1] * speed[1] + speed[2] * speed[2]
            work = speed[0] * force[0] + speed[1] * force[1] + speed[2] * force[2]
            still = solid[out_rows, :] == 1
            half_force = 1.0 - 0.5 / TAU
            base = density * (1.0 / TAU) * (1.0 - 1.5 * square) - (3.0 * half_force) * work
            scaled = density * (1.0 / TAU)
            for c in range(19):
                ex, ey, ez = VELOCITIES[c]
                keep = read[c] * (1.0 - 1.0 / TAU)
                if c == 0:
                    value = keep + WEIGHTS[0] * base
                else:
                    cu = total([e * v for e, v in zip((ex, ey, ez), speed) if e])
                    cf = total([e * v for e, v in zip((ex, ey, ez), force) if e])
                    value = keep + WEIGHTS[c] * (
                        base
                        + scaled * (cu * (3.0 + 4.5 * cu))
                        + (half_force * cf) * (3.0 + 9.0 * cu)
                    )
                new_pop[c, out_rows, :] = jnp.where(still, WEIGHTS[c], value)
            px, py, pz = gradient(order, at + PITCH)
            curve = laplace(potential, at)
            advanced = phi - (speed[0] * px + speed[1] * py + speed[2] * pz) + MOBILITY * curve
            new_order[out_rows, :] = jnp.where(still, phi, advanced)


def step(
    pop,
    phi,
    solid,
    flags,
    shift,
    site,
    direction,
    colloid,
    count,
    speed,
    slots,
    new_pop,
    new_order,
    force,
    ext,
    order,
    potential,
    out,
    below,
    above,
    south,
    north,
    up_face,
    down_face,
    high_rows,
    low_rows,
    part,
    near,
    far,
    dmap,
    wmap,
    smap,
    in_sem,
    out_sem,
    near_send,
    near_recv,
    far_send,
    far_recv,
    face_send,
    face_recv,
    row_send,
    row_recv,
):
    gx, gy = lax.axis_index("gx"), lax.axis_index("gy")
    slab_up, slab_down = lax.rem(gx + 1, 128), lax.rem(gx + 127, 128)
    z, y, x_lo = lax.rem(gx // 4, 16), lax.rem(gx, 4), gx // 64
    near_me = x_lo * 16 + y * 4 + gy

    def near_id(k):
        t = lax.rem(near_me + k, NEAR)
        return t, ((t // 16) * 64 + z * 4 + lax.rem(t // 4, 4), lax.rem(t, 4))

    def far_id(k):
        h = lax.rem(z + k, FAR)
        return h, (x_lo * 64 + h * 4 + y, gy)

    barrier = pltpu.get_barrier_semaphore()

    def greet(device):
        pl.semaphore_signal(barrier, inc=1, device_id=device, device_id_type=MESH)

    @pl.loop(1, FAR)
    def _(k):
        greet(far_id(k)[1])

    for slab in (slab_up, slab_down):
        for g in range(4):
            greet((slab, g))

    @pl.loop(1, NEAR)
    def _(k):
        greet(near_id(k)[1])

    loads = [
        pltpu.make_async_copy(
            pop.at[:, pl.ds(x * CY, CY), :],
            ext.at[:, pl.ds((x + 1) * PITCH + 8, CY), :],
            in_sem.at[x],
        )
        for x in range(CX)
    ]
    for x in (0, 7, 1, 2, 3, 4, 5, 6):
        loads[x].start()
    for x in range(CX):
        order[pl.ds((x + 2) * PITCH + 8, CY), :] = phi[pl.ds(x * CY, CY), :]
    plane_low = flags[gx]
    plane_high = flags[slab_up]
    for x in range(CX):
        loads[x].wait()
    first, last = PITCH + 8, 8 * PITCH + 8
    build_face(ext, phi, up_face, UP_X, last, (96, 112), -PLANE_SPEED, plane_high)
    build_face(ext, phi, down_face, DOWN_X, first, (0, 16), PLANE_SPEED, plane_low)
    build_rows(ext, phi, high_rows, UP_Y, CY - 1, (CY - 2, CY - 1))
    build_rows(ext, phi, low_rows, DOWN_Y, 0, (0, 1))
    build_links(ext, site, direction, colloid, count, speed, slots, dmap, wmap, smap, part)

    pl.semaphore_wait(barrier, FAR - 1 + 8 + NEAR - 1)

    def near_copy(k):
        t, device = near_id(k)
        return pltpu.make_async_remote_copy(
            src_ref=part.at[t],
            dst_ref=near.at[near_me],
            send_sem=near_send.at[t],
            recv_sem=near_recv.at[near_me],
            device_id=device,
            device_id_type=MESH,
        )

    def far_copy(k):
        h, device = far_id(k)
        return pltpu.make_async_remote_copy(
            src_ref=far.at[z],
            dst_ref=far.at[z],
            send_sem=far_send.at[h],
            recv_sem=far_recv.at[z],
            device_id=device,
            device_id_type=MESH,
        )

    rows = pl.ds(pl.multiple_of(gy * CY, CY), CY)
    faces = []
    for side, (src, dst, slab) in enumerate(
        ((up_face, below, slab_up), (down_face, above, slab_down))
    ):
        for g in range(4):
            faces.append(
                pltpu.make_async_remote_copy(
                    src_ref=src,
                    dst_ref=dst.at[:, rows, :],
                    send_sem=face_send.at[side, g],
                    recv_sem=face_recv.at[side, gy],
                    device_id=(slab, g),
                    device_id_type=MESH,
                )
            )
    edges = []
    for side, (src, dst, g) in enumerate(
        ((high_rows, south, lax.rem(gy + 1, 4)), (low_rows, north, lax.rem(gy + 3, 4)))
    ):
        edges.append(
            pltpu.make_async_remote_copy(
                src_ref=src,
                dst_ref=dst,
                send_sem=row_send.at[side],
                recv_sem=row_recv.at[side],
                device_id=(gx, g),
                device_id_type=MESH,
            )
        )

    @pl.loop(1, NEAR)
    def _(k):
        near_copy(k).start()

    for copy in faces:
        copy.start()
    for copy in edges:
        copy.start()

    near[near_me] = part[near_me]

    def arrived(buffer, sem, slot):
        pltpu.make_async_copy(buffer.at[slot], buffer.at[slot], sem.at[slot]).wait()

    @pl.loop(1, NEAR)
    def _(k):
        arrived(near, near_recv, lax.rem(near_me + k, NEAR))

    far[z] = total([near[t] for t in range(NEAR)])

    @pl.loop(1, FAR)
    def _(k):
        far_copy(k).start()

    for copy in edges:
        copy.wait_recv()
    for f in range(5):
        ext[UP_Y[f], pl.ds(PITCH + 7, 8, stride=PITCH), :] = south[f]
        ext[DOWN_Y[f], pl.ds(PITCH + 24, 8, stride=PITCH), :] = north[f]
    order[pl.ds(2 * PITCH + 6, 8, stride=PITCH), :] = south[5]
    order[pl.ds(2 * PITCH + 7, 8, stride=PITCH), :] = south[6]
    order[pl.ds(2 * PITCH + 24, 8, stride=PITCH), :] = north[5]
    order[pl.ds(2 * PITCH + 25, 8, stride=PITCH), :] = north[6]

    for side, dst in enumerate((below, above)):
        for g in range(4):
            block = dst.at[:, pl.ds(g * CY, CY), :]
            pltpu.make_async_copy(block, block, face_recv.at[side, g]).wait()

    for f in range(7):
        for dst in (below, above):
            for r in range(0, 24, 8):
                dst[f, pl.ds(64 + r, 8), :] = dst[f, pl.ds(r, 8), :]
    s = shift[0]
    begin_low = lax.rem(gy * CY - 2 - s * plane_low + 128, 64)
    begin_high = lax.rem(gy * CY - 2 + s * plane_high + 128, 64)
    for src, begin, components, layer, layers in (
        (below, begin_low, UP_X, 0, (0, 1)),
        (above, begin_high, DOWN_X, 9, (10, 11)),
    ):
        for f, c in enumerate(components):
            for k in (0, 8, 10):
                ext[c, pl.ds(layer * PITCH + 7 + k, 8), :] = src[f, pl.ds(begin + 1 + k, 8), :]
        for f, l in zip((5, 6), layers):
            for k in (0, 8, 12):
                order[pl.ds(l * PITCH + 6 + k, 8), :] = src[f, pl.ds(begin + k, 8), :]

    collide(ext, order, potential, solid, dmap, wmap, out, new_order)
    stores = [
        pltpu.make_async_copy(out.at[:, pl.ds(x * CY, CY), :], new_pop.at[:, pl.ds(x * CY, CY), :], out_sem.at[x])
        for x in range(CX)
    ]
    for copy in stores:
        copy.start()

    @pl.loop(1, FAR)
    def _(k):
        arrived(far, far_recv, lax.rem(z + k, FAR))

    summed = total([far[h] for h in range(FAR)])
    force[...] = pltpu.roll(summed, lax.rem(NZ - 4 * z, NZ), 1)[0:3, 0:4]

    for copy in stores:
        copy.wait()
    for copy in faces + edges:
        copy.wait_send()

    @pl.loop(1, NEAR)
    def _(k):
        near_copy(k).wait_send()

    @pl.loop(1, FAR)
    def _(k):
        far_copy(k).wait_send()


VM = pl.BlockSpec(memory_space=pltpu.VMEM)
SM = pl.BlockSpec(memory_space=pltpu.SMEM)
HB = pl.BlockSpec(memory_space=pl.ANY)


def shaped(*dims, dtype=F32):
    return jax.ShapeDtypeStruct(dims, dtype)


def per_device(
    populations,
    order_field,
    solid_flags,
    plane_flags,
    shear_shift,
    link_site,
    link_dir,
    link_colloid,
    link_count,
    colloid_slot,
    colloid_speed,
):
    new_pop, new_order, force = pl.pallas_call(
        step,
        out_shape=(shaped(19, ROWS, NZ), shaped(ROWS, NZ), shaped(3, 4)),
        in_specs=[HB, VM, VM, SM, SM, VM, VM, VM, SM, VM, VM],
        out_specs=[HB, VM, VM],
        scratch_shapes=[
            pltpu.VMEM((19, 10 * PITCH, NZ), F32),
            pltpu.VMEM((12 * PITCH, NZ), F32),
            pltpu.VMEM((10 * PITCH, NZ), F32),
            pltpu.VMEM((19, ROWS, NZ), F32),
            pltpu.VMEM((7, 88, NZ), F32),
            pltpu.VMEM((7, 88, NZ), F32),
            pltpu.VMEM((7, 8, NZ), F32),
            pltpu.VMEM((7, 8, NZ), F32),
            pltpu.VMEM((7, CY, NZ), F32),
            pltpu.VMEM((7, CY, NZ), F32),
            pltpu.VMEM((7, 8, NZ), F32),
            pltpu.VMEM((7, 8, NZ), F32),
            pltpu.VMEM((NEAR, 4, NZ), F32),
            pltpu.VMEM((NEAR, 4, NZ), F32),
            pltpu.VMEM((FAR, 4, NZ), F32),
            pltpu.VMEM((ROWS, NZ), I32),
            pltpu.VMEM((ROWS, NZ), F32),
            pltpu.VMEM((ROWS, NZ), F32),
            pltpu.SemaphoreType.DMA((CX,)),
            pltpu.SemaphoreType.DMA((CX,)),
            pltpu.SemaphoreType.DMA((NEAR,)),
            pltpu.SemaphoreType.DMA((NEAR,)),
            pltpu.SemaphoreType.DMA((FAR,)),
            pltpu.SemaphoreType.DMA((FAR,)),
            pltpu.SemaphoreType.DMA((2, 4)),
            pltpu.SemaphoreType.DMA((2, 4)),
            pltpu.SemaphoreType.DMA((2,)),
            pltpu.SemaphoreType.DMA((2,)),
        ],
        compiler_params=pltpu.CompilerParams(collective_id=0, has_side_effects=True),
        name="step",
    )(
        populations.reshape(19, ROWS, NZ),
        order_field.reshape(ROWS, NZ),
        solid_flags.reshape(ROWS, NZ),
        plane_flags,
        shear_shift,
        link_site.reshape(8, NZ),
        link_dir.reshape(8, NZ),
        link_colloid.reshape(8, NZ),
        link_count,
        colloid_speed,
        colloid_slot.reshape(16, NZ),
    )
    return new_pop.reshape(populations.shape), new_order.reshape(order_field.shape), force


def solution(mesh):
    return jax.shard_map(
        per_device,
        mesh=mesh,
        in_specs=(
            P(None, "gx", "gy", None),
            P("gx", "gy", None),
            P("gx", "gy", None),
            P(),
            P(),
            P(("gx", "gy")),
            P(("gx", "gy")),
            P(("gx", "gy")),
            P(("gx", "gy")),
            P(),
            P(),
        ),
        out_specs=(P(None, "gx", "gy", None), P("gx", "gy", None), P(None, ("gx", "gy"))),
        check_vma=False,
    )
```

```python
import jax
import jax.numpy as jnp
from jax import lax
from jax.experimental import pallas as pl
from jax.experimental.pallas import tpu as pltpu
from jax.sharding import PartitionSpec as P

VELOCITIES = [
    [0, 0, 0],
    [1, 0, 0],
    [-1, 0, 0],
    [0, 1, 0],
    [0, -1, 0],
    [0, 0, 1],
    [0, 0, -1],
    [1, 1, 0],
    [-1, -1, 0],
    [1, -1, 0],
    [-1, 1, 0],
    [1, 0, 1],
    [-1, 0, -1],
    [1, 0, -1],
    [-1, 0, 1],
    [0, 1, 1],
    [0, -1, -1],
    [0, 1, -1],
    [0, -1, 1],
]
WEIGHTS = [1.0 / 3.0] + [1.0 / 18.0] * 6 + [1.0 / 36.0] * 12
OPPOSITE = [0, 2, 1, 4, 3, 6, 5, 8, 7, 10, 9, 12, 11, 14, 13, 16, 15, 18, 17]
UP_X = [1, 7, 9, 11, 13]
DOWN_X = [2, 8, 10, 12, 14]
UP_Y = [3, 7, 10, 15, 17]
DOWN_Y = [4, 8, 9, 16, 18]
TAU = 0.8
BULK = 0.04
KAPPA = 0.04
MOBILITY = 0.2
PLANE_SPEED = 0.05

MESH = pl.DeviceIdType.MESH
CX, CY, NZ = 8, 16, 128
ROWS = CX * CY
PITCH = 32
NEAR, FAR = 32, 16
F32 = jnp.float32
I32 = jnp.int32


def iota(shape, dim):
    return lax.broadcasted_iota(I32, shape, dim)


def total(terms):
    terms = list(terms)
    while len(terms) > 1:
        terms = [
            terms[i] + terms[i + 1] if i + 1 < len(terms) else terms[i]
            for i in range(0, len(terms), 2)
        ]
    return terms[0]


def signed(values, axis):
    plus = total([values[c] for c in range(19) if VELOCITIES[c][axis] == 1])
    minus = total([values[c] for c in range(19) if VELOCITIES[c][axis] == -1])
    return plus - minus


def lanes_of(table, index):
    return jnp.take_along_axis(table, index, axis=1, mode="promise_in_bounds")


def build_face(pop, phi, out, components, row, phi_rows, change, flag):
    for half in range(2):
        at = pl.ds(row + 8 * half, 8)
        values = [pop[c, at, :] for c in range(19)]
        density = total(values)
        momentum = [signed(values, axis) for axis in range(3)]
        on = jnp.full((8, NZ), flag, I32) == 1
        for slot, c in enumerate(components):
            ex, ey, ez = VELOCITIES[c]
            along = total([e * m for e, m in zip((ex, ey, ez), momentum) if e])
            factor = 3.0 * ey * change + (4.5 * ey * ey - 1.5) * change * change
            correction = factor * density - (3.0 * change) * momentum[1]
            if ey:
                correction = correction + (9.0 * ey * change) * along
            boosted = values[c] + WEIGHTS[c] * correction
            out[slot, pl.ds(8 * half, 8), :] = jnp.where(on, boosted, values[c])
        for slot, phi_row in zip((5, 6), phi_rows):
            out[slot, pl.ds(8 * half, 8), :] = phi[pl.ds(phi_row + 8 * half, 8), :]


def build_rows(pop, phi, out, components, y, phi_ys):
    for slot, c in enumerate(components):
        out[slot] = pop[c, pl.ds(PITCH + 8 + y, 8, stride=PITCH), :]
    for slot, py in zip((5, 6), phi_ys):
        out[slot] = phi[pl.ds(py, 8, stride=CY), :]


def build_links(pop, site, direction, colloid, count, speed, slots, dmap, wmap, smap, part):
    shape = (8, NZ)
    sub, lane = iota(shape, 0), iota(shape, 1)
    live_to = jnp.zeros(shape, I32)
    for a in range(8):
        live_to = jnp.where(sub == a, count[a], live_to)
    live = lane < live_to
    link_site, link_dir, link_colloid = site[...], direction[...], colloid[...]
    high, low = link_colloid >> 7, link_colloid & 127
    fetched = []
    for axis in range(4):
        value = None
        for h in range(16):
            if axis < 3:
                row = speed[pl.ds(axis, 1), pl.ds(h * NZ, NZ)]
            else:
                row = slots[pl.ds(h, 1), :]
            row = jnp.broadcast_to(row, shape)
            got = lanes_of(row, low)
            value = got if value is None else jnp.where(high == h, got, value)
        fetched.append(value)
    ux, uy, uz, slot = fetched
    steps = []
    for axis in range(3):
        step = jnp.zeros(shape, F32)
        for c in range(1, 19):
            if VELOCITIES[c][axis]:
                step = jnp.where(link_dir == c, float(VELOCITIES[c][axis]), step)
        steps.append(step)
    weight = jnp.where(link_dir < 7, WEIGHTS[1], WEIGHTS[7])
    moved = 6.0 * weight * (steps[0] * ux + steps[1] * uy + steps[2] * uz)
    packed = (link_site & 15) + 16 * jnp.where(live, link_dir, 0)
    for a in range(8):
        packed_row = jnp.broadcast_to(packed[a : a + 1], shape)
        moved_row = jnp.broadcast_to(moved[a : a + 1], shape)
        for half in range(2):
            rows = pl.ds(a * CY + 8 * half, 8)
            index = 8 * (sub + 8 * half) + (lane >> 4)
            code = lanes_of(packed_row, index)
            d = jnp.where((code & 15) == (lane & 15), code >> 4, 0)
            source = jnp.zeros(shape, F32)
            for c in range(1, 19):
                source = jnp.where(d == c, pop[c, pl.ds((a + 1) * PITCH + 8 + 8 * half, 8), :], source)
            dmap[rows, :] = d
            smap[rows, :] = source
            wmap[rows, :] = source - lanes_of(moved_row, index)
    link_z = link_site & 127
    source = jnp.zeros(shape, F32)
    for y in range(CY):
        got = lanes_of(smap[pl.ds(y, 8, stride=CY), :], link_z)
        source = jnp.where((lane >> 3) == y, got, source)
    momentum = jnp.where(live, 2.0 * source - moved, 0.0)
    target = (slot >> 10) * 16 + ((slot >> 2) & 15)
    column = ((slot >> 6) & 15) * 4 + (slot & 3)
    pieces = [[], [], []]
    for axis in range(3):
        left = steps[axis] * momentum
        for split in range(3):
            piece = left.astype(jnp.bfloat16).astype(F32)
            left = left - piece
            pieces[split].append(piece)
    kind = sub & 3
    left_rows, right_rows = [[], [], []], []
    big = iota((NZ, NZ), 0)
    for a in range(8):
        spread = [
            [jnp.broadcast_to(pieces[s][axis][a : a + 1], shape) for axis in range(3)]
            for s in range(3)
        ]
        pattern = [
            jnp.where(kind == 0, p[0], jnp.where(kind == 1, p[1], jnp.where(kind == 2, p[2], 0.0)))
            for p in spread
        ]
        goes = jnp.broadcast_to(target[a : a + 1], (NZ, NZ)) == (big >> 2)
        for s in range(3):
            full = jnp.broadcast_to(pattern[s][None], (16, 8, NZ)).reshape(NZ, NZ)
            left_rows[s].append(jnp.where(goes, full, 0.0).astype(jnp.bfloat16))
        right_rows.append(
            jnp.where(jnp.broadcast_to(column[a : a + 1], (NZ, NZ)) == big, 1.0, 0.0).astype(
                jnp.bfloat16
            )
        )
    left_matrix = jnp.concatenate([jnp.concatenate(r, axis=1) for r in left_rows], axis=0)
    right_matrix = jnp.concatenate(right_rows, axis=1)
    product = lax.dot_general(
        left_matrix, right_matrix, (((1,), (1,)), ((), ())), preferred_element_type=F32
    )
    product = product[0:NZ] + product[NZ : 2 * NZ] + product[2 * NZ :]
    part[...] = product.reshape(NEAR, 4, NZ)


def turn(value, step):
    return pltpu.roll(value, step % NZ, 1)


def laplace(ref, at):
    centre = ref[pl.ds(at, 8), :]
    return (
        ref[pl.ds(at + PITCH, 8), :]
        + ref[pl.ds(at - PITCH, 8), :]
        + ref[pl.ds(at + 1, 8), :]
        + ref[pl.ds(at - 1, 8), :]
        + turn(centre, -1)
        + turn(centre, 1)
        - 6.0 * centre
    )


def gradient(ref, at):
    centre = ref[pl.ds(at, 8), :]
    return (
        (ref[pl.ds(at + PITCH, 8), :] - ref[pl.ds(at - PITCH, 8), :]) * 0.5,
        (ref[pl.ds(at + 1, 8), :] - ref[pl.ds(at - 1, 8), :]) * 0.5,
        (turn(centre, -1) - turn(centre, 1)) * 0.5,
    )


def collide(ext, order, potential, solid, dmap, wmap, new_pop, new_order):
    @pl.loop(0, CX + 2)
    def _(layer):
        at = pl.multiple_of(layer * PITCH, PITCH)
        for k in (7, 15, 17):
            v = order[pl.ds(at + PITCH + k, 8), :]
            curve = laplace(order, at + PITCH + k)
            potential[pl.ds(at + k, 8), :] = BULK * (v * v * v - v) - KAPPA * curve

    @pl.loop(0, CX)
    def _(x):
        for half in range(2):
            at = pl.multiple_of((x + 1) * PITCH, PITCH) + 8 + 8 * half
            out_rows = pl.ds(pl.multiple_of(x * CY, CY) + 8 * half, 8)
            d = dmap[out_rows, :]
            w = wmap[out_rows, :]
            read = []
            for c in range(19):
                ex, ey, ez = VELOCITIES[c]
                value = ext[c, pl.ds(at - ex * PITCH - ey, 8), :]
                if ez:
                    value = turn(value, ez)
                if c:
                    value = jnp.where(d == OPPOSITE[c], w, value)
                read.append(value)
            phi = order[pl.ds(at + PITCH, 8), :]
            slopes = gradient(potential, at)
            force = [-phi * slope for slope in slopes]
            density = total(read)
            inverse = 1.0 / density
            speed = [(signed(read, axis) + 0.5 * force[axis]) * inverse for axis in range(3)]
            square = speed[0] * speed[0] + speed[1] * speed[1] + speed[2] * speed[2]
            work = speed[0] * force[0] + speed[1] * force[1] + speed[2] * force[2]
            still = solid[out_rows, :] == 1
            half_force = 1.0 - 0.5 / TAU
            base = density * (1.0 / TAU) * (1.0 - 1.5 * square) - (3.0 * half_force) * work
            scaled = density * (1.0 / TAU)
            for c in range(19):
                ex, ey, ez = VELOCITIES[c]
                keep = read[c] * (1.0 - 1.0 / TAU)
                if c == 0:
                    value = keep + WEIGHTS[0] * base
                else:
                    cu = total([e * v for e, v in zip((ex, ey, ez), speed) if e])
                    cf = total([e * v for e, v in zip((ex, ey, ez), force) if e])
                    value = keep + WEIGHTS[c] * (
                        base
                        + scaled * (cu * (3.0 + 4.5 * cu))
                        + (half_force * cf) * (3.0 + 9.0 * cu)
                    )
                new_pop[c, out_rows, :] = jnp.where(still, WEIGHTS[c], value)
            px, py, pz = gradient(order, at + PITCH)
            curve = laplace(potential, at)
            advanced = phi - (speed[0] * px + speed[1] * py + speed[2] * pz) + MOBILITY * curve
            new_order[out_rows, :] = jnp.where(still, phi, advanced)


def step(
    pop,
    phi_in,
    solid_in,
    flags_in,
    shift_in,
    site_in,
    direction_in,
    colloid_in,
    count_in,
    speed_in,
    slots_in,
    out,
    new_order,
    force,
    phi,
    solid,
    flags,
    shift,
    site,
    direction,
    colloid,
    count,
    speed,
    slots,
    ext,
    order,
    potential,
    below,
    above,
    south,
    north,
    up_face,
    down_face,
    high_rows,
    low_rows,
    part,
    near,
    far,
    dmap,
    wmap,
    smap,
    in_sem,
    near_send,
    near_recv,
    far_send,
    far_recv,
    face_send,
    face_recv,
    row_send,
    row_recv,
):
    gx, gy = lax.axis_index("gx"), lax.axis_index("gy")
    slab_up, slab_down = lax.rem(gx + 1, 128), lax.rem(gx + 127, 128)
    z, y, x_lo = lax.rem(gx // 4, 16), lax.rem(gx, 4), gx // 64
    near_me = x_lo * 16 + y * 4 + gy
    core = lax.rem(gy, 2)

    def near_id(k):
        t = lax.rem(near_me + k, NEAR)
        return t, ((t // 16) * 64 + z * 4 + lax.rem(t // 4, 4), lax.rem(t, 4))

    def far_id(k):
        h = lax.rem(z + k, FAR)
        return h, (x_lo * 64 + h * 4 + y, gy)

    barrier = pltpu.get_barrier_semaphore()

    def greet(device):
        pl.semaphore_signal(barrier, inc=1, device_id=device, device_id_type=MESH)

    @pl.loop(1, FAR)
    def _(k):
        greet(far_id(k)[1])

    for slab in (slab_up, slab_down):
        for chip in range(2):
            greet((slab, 2 * chip + core))

    @pl.loop(1, NEAR)
    def _(k):
        greet(near_id(k)[1])

    loads = [
        pltpu.make_async_copy(
            pop.at[:, pl.ds(x * CY, CY), :],
            ext.at[:, pl.ds((x + 1) * PITCH + 8, CY), :],
            in_sem.at[x],
        )
        for x in range(CX)
    ]
    small = [
        pltpu.make_async_copy(source, target, in_sem.at[CX + i])
        for i, (source, target) in enumerate(
            (
                (site_in, site),
                (direction_in, direction),
                (colloid_in, colloid),
                (count_in, count),
                (speed_in, speed),
                (slots_in, slots),
                (flags_in, flags),
                (shift_in, shift),
                (phi_in, phi),
                (solid_in, solid),
            )
        )
    ]
    for copy in small:
        copy.start()
    for x in (0, 7, 1, 2, 3, 4, 5, 6):
        loads[x].start()
    for copy in small:
        copy.wait()
    for x in range(CX):
        order[pl.ds((x + 2) * PITCH + 8, CY), :] = phi[pl.ds(x * CY, CY), :]
    plane_low = flags[gx]
    plane_high = flags[slab_up]
    for x in range(CX):
        loads[x].wait()
    first, last = PITCH + 8, 8 * PITCH + 8
    build_face(ext, phi, up_face, UP_X, last, (96, 112), -PLANE_SPEED, plane_high)
    build_face(ext, phi, down_face, DOWN_X, first, (0, 16), PLANE_SPEED, plane_low)
    build_rows(ext, phi, high_rows, UP_Y, CY - 1, (CY - 2, CY - 1))
    build_rows(ext, phi, low_rows, DOWN_Y, 0, (0, 1))
    build_links(ext, site, direction, colloid, count, speed, slots, dmap, wmap, smap, part)

    pl.semaphore_wait(barrier, FAR - 1 + 4 + NEAR - 1)

    def near_copy(k):
        t, device = near_id(k)
        return pltpu.make_async_remote_copy(
            src_ref=part.at[t],
            dst_ref=near.at[near_me],
            send_sem=near_send.at[t],
            recv_sem=near_recv.at[near_me],
            device_id=device,
            device_id_type=MESH,
        )

    def far_copy(k):
        h, device = far_id(k)
        return pltpu.make_async_remote_copy(
            src_ref=far.at[z],
            dst_ref=far.at[z],
            send_sem=far_send.at[h],
            recv_sem=far_recv.at[z],
            device_id=device,
            device_id_type=MESH,
        )

    rows = pl.ds(pl.multiple_of(gy * CY, CY), CY)
    faces = []
    for side, (src, dst, slab) in enumerate(
        ((up_face, below, slab_up), (down_face, above, slab_down))
    ):
        for chip in range(2):
            faces.append(
                pltpu.make_async_remote_copy(
                    src_ref=src,
                    dst_ref=dst.at[:, rows, :],
                    send_sem=face_send.at[side, chip],
                    recv_sem=face_recv.at[side, gy],
                    device_id=(slab, 2 * chip + core),
                    device_id_type=MESH,
                )
            )
    edges = []
    for side, (src, dst, g) in enumerate(
        ((high_rows, south, lax.rem(gy + 1, 4)), (low_rows, north, lax.rem(gy + 3, 4)))
    ):
        edges.append(
            pltpu.make_async_remote_copy(
                src_ref=src,
                dst_ref=dst,
                send_sem=row_send.at[side],
                recv_sem=row_recv.at[side],
                device_id=(gx, g),
                device_id_type=MESH,
            )
        )

    @pl.loop(1, NEAR)
    def _(k):
        near_copy(k).start()

    for copy in faces:
        copy.start()
    for copy in edges:
        copy.start()

    near[near_me] = part[near_me]

    def arrived(buffer, sem, slot):
        pltpu.make_async_copy(buffer.at[slot], buffer.at[slot], sem.at[slot]).wait()

    @pl.loop(1, NEAR)
    def _(k):
        arrived(near, near_recv, lax.rem(near_me + k, NEAR))

    far[z] = total([near[t] for t in range(NEAR)])

    @pl.loop(1, FAR)
    def _(k):
        far_copy(k).start()

    def face_block(dst, g):
        return dst.at[:, pl.ds(pl.multiple_of(g * CY, CY), CY), :]

    relays = []
    for chip in range(2):
        for side, dst in enumerate((below, above)):
            g = 2 * chip + core
            block = face_block(dst, g)
            pltpu.make_async_copy(block, block, face_recv.at[side, g]).wait()
            relays.append(
                pltpu.make_async_remote_copy(
                    src_ref=block,
                    dst_ref=block,
                    send_sem=face_send.at[side, 2 + chip],
                    recv_sem=face_recv.at[side, g],
                    device_id=(gx, gy + 1 - 2 * core),
                    device_id_type=MESH,
                )
            )
            relays[-1].start()

    for copy in edges:
        copy.wait_recv()
    for f in range(5):
        ext[UP_Y[f], pl.ds(PITCH + 7, 8, stride=PITCH), :] = south[f]
        ext[DOWN_Y[f], pl.ds(PITCH + 24, 8, stride=PITCH), :] = north[f]
    order[pl.ds(2 * PITCH + 6, 8, stride=PITCH), :] = south[5]
    order[pl.ds(2 * PITCH + 7, 8, stride=PITCH), :] = south[6]
    order[pl.ds(2 * PITCH + 24, 8, stride=PITCH), :] = north[5]
    order[pl.ds(2 * PITCH + 25, 8, stride=PITCH), :] = north[6]

    for chip in range(2):
        for side, dst in enumerate((below, above)):
            g = 2 * chip + 1 - core
            block = face_block(dst, g)
            pltpu.make_async_copy(block, block, face_recv.at[side, g]).wait()

    for f in range(7):
        for dst in (below, above):
            for r in range(0, 24, 8):
                dst[f, pl.ds(64 + r, 8), :] = dst[f, pl.ds(r, 8), :]
    s = shift[0, 0]
    begin_low = lax.rem(gy * CY - 2 - s * plane_low + 128, 64)
    begin_high = lax.rem(gy * CY - 2 + s * plane_high + 128, 64)
    for src, begin, components, layer, layers in (
        (below, begin_low, UP_X, 0, (0, 1)),
        (above, begin_high, DOWN_X, 9, (10, 11)),
    ):
        for f, c in enumerate(components):
            for k in (0, 8, 10):
                ext[c, pl.ds(layer * PITCH + 7 + k, 8), :] = src[f, pl.ds(begin + 1 + k, 8), :]
        for f, l in zip((5, 6), layers):
            for k in (0, 8, 12):
                order[pl.ds(l * PITCH + 6 + k, 8), :] = src[f, pl.ds(begin + k, 8), :]

    collide(ext, order, potential, solid, dmap, wmap, out, new_order)
    @pl.loop(1, FAR)
    def _(k):
        arrived(far, far_recv, lax.rem(z + k, FAR))

    summed = total([far[h] for h in range(FAR)])
    force[0:4, :] = pltpu.roll(summed, lax.rem(NZ - 4 * z, NZ), 1)

    for copy in faces + edges + relays:
        copy.wait_send()

    @pl.loop(1, NEAR)
    def _(k):
        near_copy(k).wait_send()

    @pl.loop(1, FAR)
    def _(k):
        far_copy(k).wait_send()


def write(pop, order, force, new_pop, new_order, new_force, sem):
    parts = [(0, 5), (5, 5), (10, 5), (15, 4)]
    copies = [
        pltpu.make_async_copy(pop.at[pl.ds(c, n)], new_pop.at[pl.ds(c, n)], sem.at[i])
        for i, (c, n) in enumerate(parts)
    ]
    copies.append(pltpu.make_async_copy(order, new_order, sem.at[4]))
    for copy in copies:
        copy.start()
    new_force[...] = force[0:3, 0:4]
    for copy in copies:
        copy.wait()


VM = pl.BlockSpec(memory_space=pltpu.VMEM)
SM = pl.BlockSpec(memory_space=pltpu.SMEM)
HB = pl.BlockSpec(memory_space=pltpu.HBM)


def shaped(*dims, dtype=F32):
    return jax.ShapeDtypeStruct(dims, dtype)


def per_device(
    populations,
    order_field,
    solid_flags,
    plane_flags,
    shear_shift,
    link_site,
    link_dir,
    link_colloid,
    link_count,
    colloid_slot,
    colloid_speed,
):
    new_pop, new_order, force = pl.pallas_call(
        step,
        out_shape=(
            pltpu.VMEM((19, ROWS, NZ), F32),
            pltpu.VMEM((ROWS, NZ), F32),
            pltpu.VMEM((8, NZ), F32),
        ),
        in_specs=[HB] * 11,
        out_specs=[VM] * 3,
        scratch_shapes=[
            pltpu.VMEM((ROWS, NZ), F32),
            pltpu.VMEM((ROWS, NZ), I32),
            pltpu.SMEM((128,), I32),
            pltpu.SMEM((1, 1), I32),
            pltpu.VMEM((8, NZ), I32),
            pltpu.VMEM((8, NZ), I32),
            pltpu.VMEM((8, NZ), I32),
            pltpu.SMEM((8,), I32),
            pltpu.VMEM((3, 2048), F32),
            pltpu.VMEM((16, NZ), I32),
            pltpu.VMEM((19, 10 * PITCH, NZ), F32),
            pltpu.VMEM((12 * PITCH, NZ), F32),
            pltpu.VMEM((10 * PITCH, NZ), F32),
            pltpu.VMEM((7, 88, NZ), F32),
            pltpu.VMEM((7, 88, NZ), F32),
            pltpu.VMEM((7, 8, NZ), F32),
            pltpu.VMEM((7, 8, NZ), F32),
            pltpu.VMEM((7, CY, NZ), F32),
            pltpu.VMEM((7, CY, NZ), F32),
            pltpu.VMEM((7, 8, NZ), F32),
            pltpu.VMEM((7, 8, NZ), F32),
            pltpu.VMEM((NEAR, 4, NZ), F32),
            pltpu.VMEM((NEAR, 4, NZ), F32),
            pltpu.VMEM((FAR, 4, NZ), F32),
            pltpu.VMEM((ROWS, NZ), I32),
            pltpu.VMEM((ROWS, NZ), F32),
            pltpu.VMEM((ROWS, NZ), F32),
            pltpu.SemaphoreType.DMA((CX + 10,)),
            pltpu.SemaphoreType.DMA((NEAR,)),
            pltpu.SemaphoreType.DMA((NEAR,)),
            pltpu.SemaphoreType.DMA((FAR,)),
            pltpu.SemaphoreType.DMA((FAR,)),
            pltpu.SemaphoreType.DMA((2, 4)),
            pltpu.SemaphoreType.DMA((2, 4)),
            pltpu.SemaphoreType.DMA((2,)),
            pltpu.SemaphoreType.DMA((2,)),
        ],
        compiler_params=pltpu.CompilerParams(collective_id=0, has_side_effects=True),
        name="step",
    )(
        populations.reshape(19, ROWS, NZ),
        order_field.reshape(ROWS, NZ),
        solid_flags.reshape(ROWS, NZ),
        plane_flags,
        shear_shift.reshape(1, 1),
        link_site.reshape(8, NZ),
        link_dir.reshape(8, NZ),
        link_colloid.reshape(8, NZ),
        link_count,
        colloid_speed,
        colloid_slot.reshape(16, NZ),
    )
    new_pop, new_order, force = pl.pallas_call(
        write,
        out_shape=(shaped(19, ROWS, NZ), shaped(ROWS, NZ), shaped(3, 4)),
        in_specs=[VM] * 3,
        out_specs=[HB, HB, VM],
        scratch_shapes=[pltpu.SemaphoreType.DMA((5,))],
        name="write",
    )(*[pltpu.with_memory_space_constraint(v, pltpu.VMEM) for v in (new_pop, new_order, force)])
    return new_pop.reshape(populations.shape), new_order.reshape(order_field.shape), force


def solution(mesh):
    return jax.shard_map(
        per_device,
        mesh=mesh,
        in_specs=(
            P(None, "gx", "gy", None),
            P("gx", "gy", None),
            P("gx", "gy", None),
            P(),
            P(),
            P(("gx", "gy")),
            P(("gx", "gy")),
            P(("gx", "gy")),
            P(("gx", "gy")),
            P(),
            P(),
        ),
        out_specs=(P(None, "gx", "gy", None), P("gx", "gy", None), P(None, ("gx", "gy"))),
        check_vma=False,
    )
```

```python
import jax
import jax.numpy as jnp
from jax import lax
from jax.experimental import pallas as pl
from jax.experimental.pallas import tpu as pltpu
from jax.sharding import PartitionSpec as P

VELOCITIES = [
    [0, 0, 0],
    [1, 0, 0],
    [-1, 0, 0],
    [0, 1, 0],
    [0, -1, 0],
    [0, 0, 1],
    [0, 0, -1],
    [1, 1, 0],
    [-1, -1, 0],
    [1, -1, 0],
    [-1, 1, 0],
    [1, 0, 1],
    [-1, 0, -1],
    [1, 0, -1],
    [-1, 0, 1],
    [0, 1, 1],
    [0, -1, -1],
    [0, 1, -1],
    [0, -1, 1],
]
WEIGHTS = [1.0 / 3.0] + [1.0 / 18.0] * 6 + [1.0 / 36.0] * 12
OPPOSITE = [0, 2, 1, 4, 3, 6, 5, 8, 7, 10, 9, 12, 11, 14, 13, 16, 15, 18, 17]
UP_X = [1, 7, 9, 11, 13]
DOWN_X = [2, 8, 10, 12, 14]
UP_Y = [3, 7, 10, 15, 17]
DOWN_Y = [4, 8, 9, 16, 18]
TAU = 0.8
BULK = 0.04
KAPPA = 0.04
MOBILITY = 0.2
PLANE_SPEED = 0.05

MESH = pl.DeviceIdType.MESH
CX, CY, NZ = 8, 16, 128
ROWS = CX * CY
PITCH = 32
NEAR, FAR = 32, 16
F32 = jnp.float32
I32 = jnp.int32


def iota(shape, dim):
    return lax.broadcasted_iota(I32, shape, dim)


def total(terms):
    terms = list(terms)
    while len(terms) > 1:
        terms = [
            terms[i] + terms[i + 1] if i + 1 < len(terms) else terms[i]
            for i in range(0, len(terms), 2)
        ]
    return terms[0]


def signed(values, axis):
    plus = total([values[c] for c in range(19) if VELOCITIES[c][axis] == 1])
    minus = total([values[c] for c in range(19) if VELOCITIES[c][axis] == -1])
    return plus - minus


def lanes_of(table, index):
    return jnp.take_along_axis(table, index, axis=1, mode="promise_in_bounds")


def build_face(pop, phi, out, components, row, phi_rows, change, flag):
    for half in range(2):
        at = pl.ds(row + 8 * half, 8)
        values = [pop[c, at, :] for c in range(19)]
        density = total(values)
        momentum = [signed(values, axis) for axis in range(3)]
        on = jnp.full((8, NZ), flag, I32) == 1
        for slot, c in enumerate(components):
            ex, ey, ez = VELOCITIES[c]
            along = total([e * m for e, m in zip((ex, ey, ez), momentum) if e])
            factor = 3.0 * ey * change + (4.5 * ey * ey - 1.5) * change * change
            correction = factor * density - (3.0 * change) * momentum[1]
            if ey:
                correction = correction + (9.0 * ey * change) * along
            boosted = values[c] + WEIGHTS[c] * correction
            out[slot, pl.ds(8 * half, 8), :] = jnp.where(on, boosted, values[c])
        for slot, phi_row in zip((5, 6), phi_rows):
            out[slot, pl.ds(8 * half, 8), :] = phi[pl.ds(phi_row + 8 * half, 8), :]


def build_rows(pop, phi, out, components, y, phi_ys):
    for slot, c in enumerate(components):
        out[slot] = pop[c, pl.ds(PITCH + 8 + y, 8, stride=PITCH), :]
    for slot, py in zip((5, 6), phi_ys):
        out[slot] = phi[pl.ds(py, 8, stride=CY), :]


def build_links(pop, site, direction, colloid, count, speed, slots, dmap, wmap, smap, part):
    shape = (8, NZ)
    sub, lane = iota(shape, 0), iota(shape, 1)
    live_to = jnp.zeros(shape, I32)
    for a in range(8):
        live_to = jnp.where(sub == a, count[a], live_to)
    live = lane < live_to
    link_site, link_dir, link_colloid = site[...], direction[...], colloid[...]
    high, low = link_colloid >> 7, link_colloid & 127
    fetched = []
    for axis in range(4):
        value = None
        for h in range(16):
            if axis < 3:
                row = speed[pl.ds(axis, 1), pl.ds(h * NZ, NZ)]
            else:
                row = slots[pl.ds(h, 1), :]
            row = jnp.broadcast_to(row, shape)
            got = lanes_of(row, low)
            value = got if value is None else jnp.where(high == h, got, value)
        fetched.append(value)
    ux, uy, uz, slot = fetched
    steps = []
    for axis in range(3):
        step = jnp.zeros(shape, F32)
        for c in range(1, 19):
            if VELOCITIES[c][axis]:
                step = jnp.where(link_dir == c, float(VELOCITIES[c][axis]), step)
        steps.append(step)
    weight = jnp.where(link_dir < 7, WEIGHTS[1], WEIGHTS[7])
    moved = 6.0 * weight * (steps[0] * ux + steps[1] * uy + steps[2] * uz)
    packed = (link_site & 15) + 16 * jnp.where(live, link_dir, 0)
    for a in range(8):
        packed_row = jnp.broadcast_to(packed[a : a + 1], shape)
        moved_row = jnp.broadcast_to(moved[a : a + 1], shape)
        for half in range(2):
            rows = pl.ds(a * CY + 8 * half, 8)
            index = 8 * (sub + 8 * half) + (lane >> 4)
            code = lanes_of(packed_row, index)
            d = jnp.where((code & 15) == (lane & 15), code >> 4, 0)
            source = jnp.zeros(shape, F32)
            for c in range(1, 19):
                source = jnp.where(d == c, pop[c, pl.ds((a + 1) * PITCH + 8 + 8 * half, 8), :], source)
            dmap[rows, :] = d
            smap[rows, :] = source
            wmap[rows, :] = source - lanes_of(moved_row, index)
    link_z = link_site & 127
    source = jnp.zeros(shape, F32)
    for y in range(CY):
        got = lanes_of(smap[pl.ds(y, 8, stride=CY), :], link_z)
        source = jnp.where((lane >> 3) == y, got, source)
    momentum = jnp.where(live, 2.0 * source - moved, 0.0)
    target = (slot >> 10) * 16 + ((slot >> 2) & 15)
    column = ((slot >> 6) & 15) * 4 + (slot & 3)
    pieces = [[], [], []]
    for axis in range(3):
        left = steps[axis] * momentum
        for split in range(3):
            piece = left.astype(jnp.bfloat16).astype(F32)
            left = left - piece
            pieces[split].append(piece)
    kind = sub & 3
    left_rows, right_rows = [[], [], []], []
    big = iota((NZ, NZ), 0)
    for a in range(8):
        spread = [
            [jnp.broadcast_to(pieces[s][axis][a : a + 1], shape) for axis in range(3)]
            for s in range(3)
        ]
        pattern = [
            jnp.where(kind == 0, p[0], jnp.where(kind == 1, p[1], jnp.where(kind == 2, p[2], 0.0)))
            for p in spread
        ]
        goes = jnp.broadcast_to(target[a : a + 1], (NZ, NZ)) == (big >> 2)
        for s in range(3):
            full = jnp.broadcast_to(pattern[s][None], (16, 8, NZ)).reshape(NZ, NZ)
            left_rows[s].append(jnp.where(goes, full, 0.0).astype(jnp.bfloat16))
        right_rows.append(
            jnp.where(jnp.broadcast_to(column[a : a + 1], (NZ, NZ)) == big, 1.0, 0.0).astype(
                jnp.bfloat16
            )
        )
    left_matrix = jnp.concatenate([jnp.concatenate(r, axis=1) for r in left_rows], axis=0)
    right_matrix = jnp.concatenate(right_rows, axis=1)
    product = lax.dot_general(
        left_matrix, right_matrix, (((1,), (1,)), ((), ())), preferred_element_type=F32
    )
    product = product[0:NZ] + product[NZ : 2 * NZ] + product[2 * NZ :]
    part[...] = product.reshape(NEAR, 4, NZ)


def turn(value, step):
    return pltpu.roll(value, step % NZ, 1)


def laplace(ref, at):
    centre = ref[pl.ds(at, 8), :]
    return (
        ref[pl.ds(at + PITCH, 8), :]
        + ref[pl.ds(at - PITCH, 8), :]
        + ref[pl.ds(at + 1, 8), :]
        + ref[pl.ds(at - 1, 8), :]
        + turn(centre, -1)
        + turn(centre, 1)
        - 6.0 * centre
    )


def gradient(ref, at):
    centre = ref[pl.ds(at, 8), :]
    return (
        (ref[pl.ds(at + PITCH, 8), :] - ref[pl.ds(at - PITCH, 8), :]) * 0.5,
        (ref[pl.ds(at + 1, 8), :] - ref[pl.ds(at - 1, 8), :]) * 0.5,
        (turn(centre, -1) - turn(centre, 1)) * 0.5,
    )


def collide(ext, order, potential, solid, dmap, wmap, new_pop, new_order):
    @pl.loop(0, CX + 2)
    def _(layer):
        at = pl.multiple_of(layer * PITCH, PITCH)
        for k in (7, 15, 17):
            v = order[pl.ds(at + PITCH + k, 8), :]
            curve = laplace(order, at + PITCH + k)
            potential[pl.ds(at + k, 8), :] = BULK * (v * v * v - v) - KAPPA * curve

    @pl.loop(0, CX)
    def _(x):
        for half in range(2):
            at = pl.multiple_of((x + 1) * PITCH, PITCH) + 8 + 8 * half
            out_rows = pl.ds(pl.multiple_of(x * CY, CY) + 8 * half, 8)
            d = dmap[out_rows, :]
            w = wmap[out_rows, :]
            read = []
            for c in range(19):
                ex, ey, ez = VELOCITIES[c]
                value = ext[c, pl.ds(at - ex * PITCH - ey, 8), :]
                if ez:
                    value = turn(value, ez)
                if c:
                    value = jnp.where(d == OPPOSITE[c], w, value)
                read.append(value)
            phi = order[pl.ds(at + PITCH, 8), :]
            slopes = gradient(potential, at)
            force = [-phi * slope for slope in slopes]
            density = total(read)
            inverse = 1.0 / density
            speed = [(signed(read, axis) + 0.5 * force[axis]) * inverse for axis in range(3)]
            square = speed[0] * speed[0] + speed[1] * speed[1] + speed[2] * speed[2]
            work = speed[0] * force[0] + speed[1] * force[1] + speed[2] * force[2]
            still = solid[out_rows, :] == 1
            half_force = 1.0 - 0.5 / TAU
            base = density * (1.0 / TAU) * (1.0 - 1.5 * square) - (3.0 * half_force) * work
            scaled = density * (1.0 / TAU)
            for c in range(19):
                ex, ey, ez = VELOCITIES[c]
                keep = read[c] * (1.0 - 1.0 / TAU)
                if c == 0:
                    value = keep + WEIGHTS[0] * base
                else:
                    cu = total([e * v for e, v in zip((ex, ey, ez), speed) if e])
                    cf = total([e * v for e, v in zip((ex, ey, ez), force) if e])
                    value = keep + WEIGHTS[c] * (
                        base
                        + scaled * (cu * (3.0 + 4.5 * cu))
                        + (half_force * cf) * (3.0 + 9.0 * cu)
                    )
                new_pop[c, out_rows, :] = jnp.where(still, WEIGHTS[c], value)
            px, py, pz = gradient(order, at + PITCH)
            curve = laplace(potential, at)
            advanced = phi - (speed[0] * px + speed[1] * py + speed[2] * pz) + MOBILITY * curve
            new_order[out_rows, :] = jnp.where(still, phi, advanced)


def step(
    pop,
    phi_in,
    solid_in,
    flags_in,
    shift_in,
    site_in,
    direction_in,
    colloid_in,
    count_in,
    speed_in,
    slots_in,
    out,
    new_order,
    force,
    phi,
    solid,
    flags,
    shift,
    site,
    direction,
    colloid,
    count,
    speed,
    slots,
    ext,
    order,
    potential,
    below,
    above,
    south,
    north,
    up_face,
    down_face,
    high_rows,
    low_rows,
    part,
    near,
    far,
    dmap,
    wmap,
    smap,
    in_sem,
    near_send,
    near_recv,
    far_send,
    far_recv,
    face_send,
    face_recv,
    row_send,
    row_recv,
    told,
):
    gx, gy = lax.axis_index("gx"), lax.axis_index("gy")
    slab_up, slab_down = lax.rem(gx + 1, 128), lax.rem(gx + 127, 128)
    z, y, x_lo = lax.rem(gx // 4, 16), lax.rem(gx, 4), gx // 64
    near_me = x_lo * 16 + y * 4 + gy
    core = lax.rem(gy, 2)
    chip_x = gy // 2

    peers = []
    for flip_x in range(2):
        for step_y in range(4):
            for flip_chip in range(2):
                for flip_core in range(2):
                    hops = min(step_y, 4 - step_y) + (1 if flip_x else 2 * flip_chip)
                    peers.append((-hops, flip_x, step_y, flip_chip, flip_core))
    peers = [p[1:] for p in sorted(peers) if any(p[1:])]

    def near_id(peer):
        flip_x, step_y, flip_chip, flip_core = peer
        to_x = 1 - x_lo if flip_x else x_lo
        to_y = lax.rem(y + step_y, 4)
        to_chip = 1 - chip_x if flip_chip else chip_x
        to_core = 1 - core if flip_core else core
        to_gy = 2 * to_chip + to_core
        return to_x * 16 + to_y * 4 + to_gy, (to_x * 64 + z * 4 + to_y, to_gy)

    def far_id(k):
        h = lax.rem(z + k, FAR)
        return h, (x_lo * 64 + h * 4 + y, gy)

    barrier = pltpu.get_barrier_semaphore()

    def greet(device):
        pl.semaphore_signal(barrier, inc=1, device_id=device, device_id_type=MESH)

    def along(k):
        return (x_lo * 64 + lax.rem(z + k + FAR, FAR) * 4 + y, gy)

    for k in (4, -4, 3, -3, 2, -2, 1, -1):
        greet(along(k))

    for slab in (slab_up, slab_down):
        for chip in range(2):
            greet((slab, 2 * chip + core))

    for peer in peers:
        greet(near_id(peer)[1])

    loads = [
        pltpu.make_async_copy(
            pop.at[:, pl.ds(x * CY, CY), :],
            ext.at[:, pl.ds((x + 1) * PITCH + 8, CY), :],
            in_sem.at[x],
        )
        for x in range(CX)
    ]
    small = [
        pltpu.make_async_copy(source, target, in_sem.at[CX + i])
        for i, (source, target) in enumerate(
            (
                (site_in, site),
                (direction_in, direction),
                (colloid_in, colloid),
                (count_in, count),
                (speed_in, speed),
                (slots_in, slots),
                (flags_in, flags),
                (shift_in, shift),
                (phi_in, phi),
                (solid_in, solid),
            )
        )
    ]
    for copy in small:
        copy.start()
    for x in (0, 7, 1, 2, 3, 4, 5, 6):
        loads[x].start()
    for copy in small:
        copy.wait()
    for x in range(CX):
        order[pl.ds((x + 2) * PITCH + 8, CY), :] = phi[pl.ds(x * CY, CY), :]
    plane_low = flags[gx]
    plane_high = flags[slab_up]
    for x in range(CX):
        loads[x].wait()
    first, last = PITCH + 8, 8 * PITCH + 8
    build_face(ext, phi, up_face, UP_X, last, (96, 112), -PLANE_SPEED, plane_high)
    build_face(ext, phi, down_face, DOWN_X, first, (0, 16), PLANE_SPEED, plane_low)
    build_rows(ext, phi, high_rows, UP_Y, CY - 1, (CY - 2, CY - 1))
    build_rows(ext, phi, low_rows, DOWN_Y, 0, (0, 1))
    build_links(ext, site, direction, colloid, count, speed, slots, dmap, wmap, smap, part)

    pl.semaphore_wait(barrier, 8 + 4 + NEAR - 1)

    def near_copy(k):
        t, device = near_id(k)
        return pltpu.make_async_remote_copy(
            src_ref=part.at[t],
            dst_ref=near.at[near_me],
            send_sem=near_send.at[t],
            recv_sem=near_recv.at[near_me],
            device_id=device,
            device_id_type=MESH,
        )

    def far_copy(k):
        h, device = far_id(k)
        return pltpu.make_async_remote_copy(
            src_ref=far.at[z],
            dst_ref=far.at[z],
            send_sem=far_send.at[h],
            recv_sem=far_recv.at[z],
            device_id=device,
            device_id_type=MESH,
        )

    rows = pl.ds(pl.multiple_of(gy * CY, CY), CY)
    faces = []
    for side, (src, dst, slab) in enumerate(
        ((up_face, below, slab_up), (down_face, above, slab_down))
    ):
        for chip in range(2):
            faces.append(
                pltpu.make_async_remote_copy(
                    src_ref=src,
                    dst_ref=dst.at[:, rows, :],
                    send_sem=face_send.at[side, chip],
                    recv_sem=face_recv.at[side, gy],
                    device_id=(slab, 2 * chip + core),
                    device_id_type=MESH,
                )
            )
    edges = []
    for side, (src, dst, g) in enumerate(
        ((high_rows, south, lax.rem(gy + 1, 4)), (low_rows, north, lax.rem(gy + 3, 4)))
    ):
        edges.append(
            pltpu.make_async_remote_copy(
                src_ref=src,
                dst_ref=dst,
                send_sem=row_send.at[side],
                recv_sem=row_recv.at[side],
                device_id=(gx, g),
                device_id_type=MESH,
            )
        )

    for device in (along(4), along(-4)):
        pl.semaphore_signal(told, inc=1, device_id=device, device_id_type=MESH)
    for peer in peers:
        near_copy(peer).start()

    for copy in faces:
        copy.start()
    for copy in edges:
        copy.start()

    near[near_me] = part[near_me]

    def arrived(buffer, sem, slot):
        pltpu.make_async_copy(buffer.at[slot], buffer.at[slot], sem.at[slot]).wait()

    for peer in peers[::-1]:
        arrived(near, near_recv, near_id(peer)[0])

    far[z] = total([near[t] for t in range(NEAR)])

    pl.semaphore_wait(told, 2)
    for k in (8, 7, 9, 6, 10, 5, 11, 4, 12, 3, 13, 2, 14, 1, 15):
        far_copy(k).start()

    def face_block(dst, g):
        return dst.at[:, pl.ds(pl.multiple_of(g * CY, CY), CY), :]

    relays = []
    for chip in range(2):
        for side, dst in enumerate((below, above)):
            g = 2 * chip + core
            block = face_block(dst, g)
            pltpu.make_async_copy(block, block, face_recv.at[side, g]).wait()
            relays.append(
                pltpu.make_async_remote_copy(
                    src_ref=block,
                    dst_ref=block,
                    send_sem=face_send.at[side, 2 + chip],
                    recv_sem=face_recv.at[side, g],
                    device_id=(gx, gy + 1 - 2 * core),
                    device_id_type=MESH,
                )
            )
            relays[-1].start()

    for copy in edges:
        copy.wait_recv()
    for f in range(5):
        ext[UP_Y[f], pl.ds(PITCH + 7, 8, stride=PITCH), :] = south[f]
        ext[DOWN_Y[f], pl.ds(PITCH + 24, 8, stride=PITCH), :] = north[f]
    order[pl.ds(2 * PITCH + 6, 8, stride=PITCH), :] = south[5]
    order[pl.ds(2 * PITCH + 7, 8, stride=PITCH), :] = south[6]
    order[pl.ds(2 * PITCH + 24, 8, stride=PITCH), :] = north[5]
    order[pl.ds(2 * PITCH + 25, 8, stride=PITCH), :] = north[6]

    for chip in range(2):
        for side, dst in enumerate((below, above)):
            g = 2 * chip + 1 - core
            block = face_block(dst, g)
            pltpu.make_async_copy(block, block, face_recv.at[side, g]).wait()

    for f in range(7):
        for dst in (below, above):
            for r in range(0, 24, 8):
                dst[f, pl.ds(64 + r, 8), :] = dst[f, pl.ds(r, 8), :]
    s = shift[0, 0]
    begin_low = lax.rem(gy * CY - 2 - s * plane_low + 128, 64)
    begin_high = lax.rem(gy * CY - 2 + s * plane_high + 128, 64)
    for src, begin, components, layer, layers in (
        (below, begin_low, UP_X, 0, (0, 1)),
        (above, begin_high, DOWN_X, 9, (10, 11)),
    ):
        for f, c in enumerate(components):
            for k in (0, 8, 10):
                ext[c, pl.ds(layer * PITCH + 7 + k, 8), :] = src[f, pl.ds(begin + 1 + k, 8), :]
        for f, l in zip((5, 6), layers):
            for k in (0, 8, 12):
                order[pl.ds(l * PITCH + 6 + k, 8), :] = src[f, pl.ds(begin + k, 8), :]

    collide(ext, order, potential, solid, dmap, wmap, out, new_order)
    @pl.loop(1, FAR)
    def _(k):
        arrived(far, far_recv, lax.rem(z + k, FAR))

    summed = total([far[h] for h in range(FAR)])
    force[0:4, :] = pltpu.roll(summed, lax.rem(NZ - 4 * z, NZ), 1)

    for copy in faces + edges + relays:
        copy.wait_send()

    for peer in peers:
        near_copy(peer).wait_send()

    @pl.loop(1, FAR)
    def _(k):
        far_copy(k).wait_send()


def write(pop, order, force, new_pop, new_order, new_force, sem):
    parts = [(0, 5), (5, 5), (10, 5), (15, 4)]
    copies = [
        pltpu.make_async_copy(pop.at[pl.ds(c, n)], new_pop.at[pl.ds(c, n)], sem.at[i])
        for i, (c, n) in enumerate(parts)
    ]
    copies.append(pltpu.make_async_copy(order, new_order, sem.at[4]))
    for copy in copies:
        copy.start()
    new_force[...] = force[0:3, 0:4]
    for copy in copies:
        copy.wait()


VM = pl.BlockSpec(memory_space=pltpu.VMEM)
SM = pl.BlockSpec(memory_space=pltpu.SMEM)
HB = pl.BlockSpec(memory_space=pltpu.HBM)


def shaped(*dims, dtype=F32):
    return jax.ShapeDtypeStruct(dims, dtype)


def per_device(
    populations,
    order_field,
    solid_flags,
    plane_flags,
    shear_shift,
    link_site,
    link_dir,
    link_colloid,
    link_count,
    colloid_slot,
    colloid_speed,
):
    new_pop, new_order, force = pl.pallas_call(
        step,
        out_shape=(
            pltpu.VMEM((19, ROWS, NZ), F32),
            pltpu.VMEM((ROWS, NZ), F32),
            pltpu.VMEM((8, NZ), F32),
        ),
        in_specs=[HB] * 11,
        out_specs=[VM] * 3,
        scratch_shapes=[
            pltpu.VMEM((ROWS, NZ), F32),
            pltpu.VMEM((ROWS, NZ), I32),
            pltpu.SMEM((128,), I32),
            pltpu.SMEM((1, 1), I32),
            pltpu.VMEM((8, NZ), I32),
            pltpu.VMEM((8, NZ), I32),
            pltpu.VMEM((8, NZ), I32),
            pltpu.SMEM((8,), I32),
            pltpu.VMEM((3, 2048), F32),
            pltpu.VMEM((16, NZ), I32),
            pltpu.VMEM((19, 10 * PITCH, NZ), F32),
            pltpu.VMEM((12 * PITCH, NZ), F32),
            pltpu.VMEM((10 * PITCH, NZ), F32),
            pltpu.VMEM((7, 88, NZ), F32),
            pltpu.VMEM((7, 88, NZ), F32),
            pltpu.VMEM((7, 8, NZ), F32),
            pltpu.VMEM((7, 8, NZ), F32),
            pltpu.VMEM((7, CY, NZ), F32),
            pltpu.VMEM((7, CY, NZ), F32),
            pltpu.VMEM((7, 8, NZ), F32),
            pltpu.VMEM((7, 8, NZ), F32),
            pltpu.VMEM((NEAR, 4, NZ), F32),
            pltpu.VMEM((NEAR, 4, NZ), F32),
            pltpu.VMEM((FAR, 4, NZ), F32),
            pltpu.VMEM((ROWS, NZ), I32),
            pltpu.VMEM((ROWS, NZ), F32),
            pltpu.VMEM((ROWS, NZ), F32),
            pltpu.SemaphoreType.DMA((CX + 10,)),
            pltpu.SemaphoreType.DMA((NEAR,)),
            pltpu.SemaphoreType.DMA((NEAR,)),
            pltpu.SemaphoreType.DMA((FAR,)),
            pltpu.SemaphoreType.DMA((FAR,)),
            pltpu.SemaphoreType.DMA((2, 4)),
            pltpu.SemaphoreType.DMA((2, 4)),
            pltpu.SemaphoreType.DMA((2,)),
            pltpu.SemaphoreType.DMA((2,)),
            pltpu.SemaphoreType.REGULAR,
        ],
        compiler_params=pltpu.CompilerParams(collective_id=0, has_side_effects=True),
        name="step",
    )(
        populations.reshape(19, ROWS, NZ),
        order_field.reshape(ROWS, NZ),
        solid_flags.reshape(ROWS, NZ),
        plane_flags,
        shear_shift.reshape(1, 1),
        link_site.reshape(8, NZ),
        link_dir.reshape(8, NZ),
        link_colloid.reshape(8, NZ),
        link_count,
        colloid_speed,
        colloid_slot.reshape(16, NZ),
    )
    new_pop, new_order, force = pl.pallas_call(
        write,
        out_shape=(shaped(19, ROWS, NZ), shaped(ROWS, NZ), shaped(3, 4)),
        in_specs=[VM] * 3,
        out_specs=[HB, HB, VM],
        scratch_shapes=[pltpu.SemaphoreType.DMA((5,))],
        name="write",
    )(*[pltpu.with_memory_space_constraint(v, pltpu.VMEM) for v in (new_pop, new_order, force)])
    return new_pop.reshape(populations.shape), new_order.reshape(order_field.shape), force


def solution(mesh):
    return jax.shard_map(
        per_device,
        mesh=mesh,
        in_specs=(
            P(None, "gx", "gy", None),
            P("gx", "gy", None),
            P("gx", "gy", None),
            P(),
            P(),
            P(("gx", "gy")),
            P(("gx", "gy")),
            P(("gx", "gy")),
            P(("gx", "gy")),
            P(),
            P(),
        ),
        out_specs=(P(None, "gx", "gy", None), P("gx", "gy", None), P(None, ("gx", "gy"))),
        check_vma=False,
    )
```

```python
import jax
import jax.numpy as jnp
from jax import lax
from jax.experimental import pallas as pl
from jax.experimental.pallas import tpu as pltpu
from jax.sharding import PartitionSpec as P

VELOCITIES = [
    [0, 0, 0],
    [1, 0, 0],
    [-1, 0, 0],
    [0, 1, 0],
    [0, -1, 0],
    [0, 0, 1],
    [0, 0, -1],
    [1, 1, 0],
    [-1, -1, 0],
    [1, -1, 0],
    [-1, 1, 0],
    [1, 0, 1],
    [-1, 0, -1],
    [1, 0, -1],
    [-1, 0, 1],
    [0, 1, 1],
    [0, -1, -1],
    [0, 1, -1],
    [0, -1, 1],
]
WEIGHTS = [1.0 / 3.0] + [1.0 / 18.0] * 6 + [1.0 / 36.0] * 12
OPPOSITE = [0, 2, 1, 4, 3, 6, 5, 8, 7, 10, 9, 12, 11, 14, 13, 16, 15, 18, 17]
UP_X = [1, 7, 9, 11, 13]
DOWN_X = [2, 8, 10, 12, 14]
UP_Y = [3, 7, 10, 15, 17]
DOWN_Y = [4, 8, 9, 16, 18]
TAU = 0.8
BULK = 0.04
KAPPA = 0.04
MOBILITY = 0.2
PLANE_SPEED = 0.05

MESH = pl.DeviceIdType.MESH
CX, CY, NZ = 8, 16, 128
ROWS = CX * CY
PITCH = 32
NEAR, FAR = 32, 16
F32 = jnp.float32
I32 = jnp.int32


def iota(shape, dim):
    return lax.broadcasted_iota(I32, shape, dim)


def total(terms):
    terms = list(terms)
    while len(terms) > 1:
        terms = [
            terms[i] + terms[i + 1] if i + 1 < len(terms) else terms[i]
            for i in range(0, len(terms), 2)
        ]
    return terms[0]


def signed(values, axis):
    plus = total([values[c] for c in range(19) if VELOCITIES[c][axis] == 1])
    minus = total([values[c] for c in range(19) if VELOCITIES[c][axis] == -1])
    return plus - minus


def lanes_of(table, index):
    return jnp.take_along_axis(table, index, axis=1, mode="promise_in_bounds")


def build_face(pop, phi, out, components, row, phi_rows, change, flag):
    for half in range(2):
        at = pl.ds(row + 8 * half, 8)
        values = [pop[c, at, :] for c in range(19)]
        density = total(values)
        momentum = [signed(values, axis) for axis in range(3)]
        on = jnp.full((8, NZ), flag, I32) == 1
        for slot, c in enumerate(components):
            ex, ey, ez = VELOCITIES[c]
            along = total([e * m for e, m in zip((ex, ey, ez), momentum) if e])
            factor = 3.0 * ey * change + (4.5 * ey * ey - 1.5) * change * change
            correction = factor * density - (3.0 * change) * momentum[1]
            if ey:
                correction = correction + (9.0 * ey * change) * along
            boosted = values[c] + WEIGHTS[c] * correction
            out[slot, pl.ds(8 * half, 8), :] = jnp.where(on, boosted, values[c])
        for slot, phi_row in zip((5, 6), phi_rows):
            out[slot, pl.ds(8 * half, 8), :] = phi[pl.ds(phi_row + 8 * half, 8), :]


def build_rows(pop, phi, out, components, y, phi_ys):
    for slot, c in enumerate(components):
        out[slot] = pop[c, pl.ds(PITCH + 8 + y, 8, stride=PITCH), :]
    for slot, py in zip((5, 6), phi_ys):
        out[slot] = phi[pl.ds(py, 8, stride=CY), :]


def build_links(pop, site, direction, colloid, count, speed, slots, dmap, wmap, smap, part):
    shape = (8, NZ)
    sub, lane = iota(shape, 0), iota(shape, 1)
    live_to = jnp.zeros(shape, I32)
    for a in range(8):
        live_to = jnp.where(sub == a, count[a], live_to)
    live = lane < live_to
    link_site, link_dir, link_colloid = site[...], direction[...], colloid[...]
    high, low = link_colloid >> 7, link_colloid & 127
    fetched = []
    for axis in range(4):
        value = None
        for h in range(16):
            if axis < 3:
                row = speed[pl.ds(axis, 1), pl.ds(h * NZ, NZ)]
            else:
                row = slots[pl.ds(h, 1), :]
            row = jnp.broadcast_to(row, shape)
            got = lanes_of(row, low)
            value = got if value is None else jnp.where(high == h, got, value)
        fetched.append(value)
    ux, uy, uz, slot = fetched
    steps = []
    for axis in range(3):
        step = jnp.zeros(shape, F32)
        for c in range(1, 19):
            if VELOCITIES[c][axis]:
                step = jnp.where(link_dir == c, float(VELOCITIES[c][axis]), step)
        steps.append(step)
    weight = jnp.where(link_dir < 7, WEIGHTS[1], WEIGHTS[7])
    moved = 6.0 * weight * (steps[0] * ux + steps[1] * uy + steps[2] * uz)
    packed = (link_site & 15) + 16 * jnp.where(live, link_dir, 0)
    for a in range(8):
        packed_row = jnp.broadcast_to(packed[a : a + 1], shape)
        moved_row = jnp.broadcast_to(moved[a : a + 1], shape)
        for half in range(2):
            rows = pl.ds(a * CY + 8 * half, 8)
            index = 8 * (sub + 8 * half) + (lane >> 4)
            code = lanes_of(packed_row, index)
            d = jnp.where((code & 15) == (lane & 15), code >> 4, 0)
            source = jnp.zeros(shape, F32)
            for c in range(1, 19):
                source = jnp.where(d == c, pop[c, pl.ds((a + 1) * PITCH + 8 + 8 * half, 8), :], source)
            dmap[rows, :] = d
            smap[rows, :] = source
            wmap[rows, :] = source - lanes_of(moved_row, index)
    link_z = link_site & 127
    source = jnp.zeros(shape, F32)
    for y in range(CY):
        got = lanes_of(smap[pl.ds(y, 8, stride=CY), :], link_z)
        source = jnp.where((lane >> 3) == y, got, source)
    momentum = jnp.where(live, 2.0 * source - moved, 0.0)
    target = (slot >> 10) * 16 + ((slot >> 2) & 15)
    column = ((slot >> 6) & 15) * 4 + (slot & 3)
    pieces = [[], [], []]
    for axis in range(3):
        left = steps[axis] * momentum
        for split in range(3):
            piece = left.astype(jnp.bfloat16).astype(F32)
            left = left - piece
            pieces[split].append(piece)
    even = (sub & 1) == 0
    left_rows, right_rows = [[], [], []], []
    row_of, column_of = iota((2 * NEAR, NZ), 0) >> 1, iota((NZ, NZ), 0)
    for half in range(2):
        for a in range(8):
            spread = [
                [jnp.broadcast_to(pieces[s][axis][a : a + 1], shape) for axis in range(3)]
                for s in range(3)
            ]
            goes = jnp.broadcast_to(target[a : a + 1], (2 * NEAR, NZ)) == row_of
            for s in range(3):
                if half == 0:
                    pattern = jnp.where(even, spread[s][0], spread[s][2])
                else:
                    pattern = jnp.where(even, spread[s][1], 0.0)
                full = jnp.broadcast_to(pattern[None], (8, 8, NZ)).reshape(2 * NEAR, NZ)
                left_rows[s].append(jnp.where(goes, full, 0.0).astype(jnp.bfloat16))
            lands = jnp.broadcast_to(column[a : a + 1] + 64 * half, (NZ, NZ)) == column_of
            right_rows.append(jnp.where(lands, 1.0, 0.0).astype(jnp.bfloat16))
    left_matrix = jnp.concatenate([jnp.concatenate(r, axis=1) for r in left_rows], axis=0)
    right_matrix = jnp.concatenate(right_rows, axis=1)
    product = lax.dot_general(
        left_matrix, right_matrix, (((1,), (1,)), ((), ())), preferred_element_type=F32
    )
    product = product[0:64] + product[64:128] + product[128:]
    part[...] = product.reshape(NEAR, 2, NZ)


def turn(value, step):
    return pltpu.roll(value, step % NZ, 1)


def laplace(ref, at):
    centre = ref[pl.ds(at, 8), :]
    return (
        ref[pl.ds(at + PITCH, 8), :]
        + ref[pl.ds(at - PITCH, 8), :]
        + ref[pl.ds(at + 1, 8), :]
        + ref[pl.ds(at - 1, 8), :]
        + turn(centre, -1)
        + turn(centre, 1)
        - 6.0 * centre
    )


def gradient(ref, at):
    centre = ref[pl.ds(at, 8), :]
    return (
        (ref[pl.ds(at + PITCH, 8), :] - ref[pl.ds(at - PITCH, 8), :]) * 0.5,
        (ref[pl.ds(at + 1, 8), :] - ref[pl.ds(at - 1, 8), :]) * 0.5,
        (turn(centre, -1) - turn(centre, 1)) * 0.5,
    )


def collide(ext, order, potential, solid, dmap, wmap, new_pop, new_order):
    @pl.loop(0, CX + 2)
    def _(layer):
        at = pl.multiple_of(layer * PITCH, PITCH)
        for k in (7, 15, 17):
            v = order[pl.ds(at + PITCH + k, 8), :]
            curve = laplace(order, at + PITCH + k)
            potential[pl.ds(at + k, 8), :] = BULK * (v * v * v - v) - KAPPA * curve

    @pl.loop(0, CX)
    def _(x):
        for half in range(2):
            at = pl.multiple_of((x + 1) * PITCH, PITCH) + 8 + 8 * half
            out_rows = pl.ds(pl.multiple_of(x * CY, CY) + 8 * half, 8)
            d = dmap[out_rows, :]
            w = wmap[out_rows, :]
            read = []
            for c in range(19):
                ex, ey, ez = VELOCITIES[c]
                value = ext[c, pl.ds(at - ex * PITCH - ey, 8), :]
                if ez:
                    value = turn(value, ez)
                if c:
                    value = jnp.where(d == OPPOSITE[c], w, value)
                read.append(value)
            phi = order[pl.ds(at + PITCH, 8), :]
            slopes = gradient(potential, at)
            force = [-phi * slope for slope in slopes]
            density = total(read)
            inverse = 1.0 / density
            speed = [(signed(read, axis) + 0.5 * force[axis]) * inverse for axis in range(3)]
            square = speed[0] * speed[0] + speed[1] * speed[1] + speed[2] * speed[2]
            work = speed[0] * force[0] + speed[1] * force[1] + speed[2] * force[2]
            still = solid[out_rows, :] == 1
            half_force = 1.0 - 0.5 / TAU
            base = density * (1.0 / TAU) * (1.0 - 1.5 * square) - (3.0 * half_force) * work
            scaled = density * (1.0 / TAU)
            for c in range(19):
                ex, ey, ez = VELOCITIES[c]
                keep = read[c] * (1.0 - 1.0 / TAU)
                if c == 0:
                    value = keep + WEIGHTS[0] * base
                else:
                    cu = total([e * v for e, v in zip((ex, ey, ez), speed) if e])
                    cf = total([e * v for e, v in zip((ex, ey, ez), force) if e])
                    value = keep + WEIGHTS[c] * (
                        base
                        + scaled * (cu * (3.0 + 4.5 * cu))
                        + (half_force * cf) * (3.0 + 9.0 * cu)
                    )
                new_pop[c, out_rows, :] = jnp.where(still, WEIGHTS[c], value)
            px, py, pz = gradient(order, at + PITCH)
            curve = laplace(potential, at)
            advanced = phi - (speed[0] * px + speed[1] * py + speed[2] * pz) + MOBILITY * curve
            new_order[out_rows, :] = jnp.where(still, phi, advanced)


def step(
    pop,
    phi_in,
    solid_in,
    flags_in,
    shift_in,
    site_in,
    direction_in,
    colloid_in,
    count_in,
    speed_in,
    slots_in,
    out,
    new_order,
    force,
    phi,
    solid,
    flags,
    shift,
    site,
    direction,
    colloid,
    count,
    speed,
    slots,
    ext,
    order,
    potential,
    below,
    above,
    south,
    north,
    up_face,
    down_face,
    high_rows,
    low_rows,
    part,
    near,
    far,
    dmap,
    wmap,
    smap,
    in_sem,
    near_send,
    near_recv,
    far_send,
    far_recv,
    face_send,
    face_recv,
    row_send,
    row_recv,
    told,
):
    gx, gy = lax.axis_index("gx"), lax.axis_index("gy")
    slab_up, slab_down = lax.rem(gx + 1, 128), lax.rem(gx + 127, 128)
    z, y, x_lo = lax.rem(gx // 4, 16), lax.rem(gx, 4), gx // 64
    near_me = x_lo * 16 + y * 4 + gy
    core = lax.rem(gy, 2)
    chip_x = gy // 2

    peers = []
    for flip_x in range(2):
        for step_y in range(4):
            for flip_chip in range(2):
                for flip_core in range(2):
                    hops = min(step_y, 4 - step_y) + (1 if flip_x else 2 * flip_chip)
                    peers.append((-hops, flip_x, step_y, flip_chip, flip_core))
    peers = [p[1:] for p in sorted(peers) if any(p[1:])]

    def near_id(peer):
        flip_x, step_y, flip_chip, flip_core = peer
        to_x = 1 - x_lo if flip_x else x_lo
        to_y = lax.rem(y + step_y, 4)
        to_chip = 1 - chip_x if flip_chip else chip_x
        to_core = 1 - core if flip_core else core
        to_gy = 2 * to_chip + to_core
        return to_x * 16 + to_y * 4 + to_gy, (to_x * 64 + z * 4 + to_y, to_gy)

    def far_id(k):
        h = lax.rem(z + k, FAR)
        return h, (x_lo * 64 + h * 4 + y, gy)

    barrier = pltpu.get_barrier_semaphore()

    def greet(device):
        pl.semaphore_signal(barrier, inc=1, device_id=device, device_id_type=MESH)

    def along(k):
        return (x_lo * 64 + lax.rem(z + k + FAR, FAR) * 4 + y, gy)

    for k in (4, -4, 3, -3, 2, -2, 1, -1):
        greet(along(k))

    for slab in (slab_up, slab_down):
        for chip in range(2):
            greet((slab, 2 * chip + core))

    for peer in peers:
        greet(near_id(peer)[1])

    loads = [
        pltpu.make_async_copy(
            pop.at[:, pl.ds(x * CY, CY), :],
            ext.at[:, pl.ds((x + 1) * PITCH + 8, CY), :],
            in_sem.at[x],
        )
        for x in range(CX)
    ]
    small = [
        pltpu.make_async_copy(source, target, in_sem.at[CX + i])
        for i, (source, target) in enumerate(
            (
                (site_in, site),
                (direction_in, direction),
                (colloid_in, colloid),
                (count_in, count),
                (speed_in, speed),
                (slots_in, slots),
                (flags_in, flags),
                (shift_in, shift),
                (phi_in, phi),
                (solid_in, solid),
            )
        )
    ]
    for copy in small:
        copy.start()
    for x in (0, 7, 1, 2, 3, 4, 5, 6):
        loads[x].start()
    for copy in small:
        copy.wait()
    for x in range(CX):
        order[pl.ds((x + 2) * PITCH + 8, CY), :] = phi[pl.ds(x * CY, CY), :]
    plane_low = flags[gx]
    plane_high = flags[slab_up]
    for x in range(CX):
        loads[x].wait()
    first, last = PITCH + 8, 8 * PITCH + 8
    build_face(ext, phi, up_face, UP_X, last, (96, 112), -PLANE_SPEED, plane_high)
    build_face(ext, phi, down_face, DOWN_X, first, (0, 16), PLANE_SPEED, plane_low)
    build_rows(ext, phi, high_rows, UP_Y, CY - 1, (CY - 2, CY - 1))
    build_rows(ext, phi, low_rows, DOWN_Y, 0, (0, 1))
    build_links(ext, site, direction, colloid, count, speed, slots, dmap, wmap, smap, part)

    pl.semaphore_wait(barrier, 8 + 4 + NEAR - 1)

    def near_copy(k):
        t, device = near_id(k)
        return pltpu.make_async_remote_copy(
            src_ref=part.at[t],
            dst_ref=near.at[near_me],
            send_sem=near_send.at[t],
            recv_sem=near_recv.at[near_me],
            device_id=device,
            device_id_type=MESH,
        )

    def far_copy(k):
        h, device = far_id(k)
        return pltpu.make_async_remote_copy(
            src_ref=far.at[z],
            dst_ref=far.at[z],
            send_sem=far_send.at[h],
            recv_sem=far_recv.at[z],
            device_id=device,
            device_id_type=MESH,
        )

    rows = pl.ds(pl.multiple_of(gy * CY, CY), CY)
    faces = []
    for side, (src, dst, slab) in enumerate(
        ((up_face, below, slab_up), (down_face, above, slab_down))
    ):
        for chip in range(2):
            faces.append(
                pltpu.make_async_remote_copy(
                    src_ref=src,
                    dst_ref=dst.at[:, rows, :],
                    send_sem=face_send.at[side, chip],
                    recv_sem=face_recv.at[side, gy],
                    device_id=(slab, 2 * chip + core),
                    device_id_type=MESH,
                )
            )
    edges = []
    for side, (src, dst, g) in enumerate(
        ((high_rows, south, lax.rem(gy + 1, 4)), (low_rows, north, lax.rem(gy + 3, 4)))
    ):
        edges.append(
            pltpu.make_async_remote_copy(
                src_ref=src,
                dst_ref=dst,
                send_sem=row_send.at[side],
                recv_sem=row_recv.at[side],
                device_id=(gx, g),
                device_id_type=MESH,
            )
        )

    for device in (along(4), along(-4)):
        pl.semaphore_signal(told, inc=1, device_id=device, device_id_type=MESH)
    for peer in peers:
        near_copy(peer).start()

    for copy in faces:
        copy.start()
    for copy in edges:
        copy.start()

    near[near_me] = part[near_me]

    def arrived(buffer, sem, slot):
        pltpu.make_async_copy(buffer.at[slot], buffer.at[slot], sem.at[slot]).wait()

    for peer in peers[::-1]:
        arrived(near, near_recv, near_id(peer)[0])

    far[z] = total([near[t] for t in range(NEAR)])

    pl.semaphore_wait(told, 2)
    for k in (8, 7, 9, 6, 10, 5, 11, 4, 12, 3, 13, 2, 14, 1, 15):
        far_copy(k).start()

    def face_block(dst, g):
        return dst.at[:, pl.ds(pl.multiple_of(g * CY, CY), CY), :]

    relays = []
    for chip in range(2):
        for side, dst in enumerate((below, above)):
            g = 2 * chip + core
            block = face_block(dst, g)
            pltpu.make_async_copy(block, block, face_recv.at[side, g]).wait()
            relays.append(
                pltpu.make_async_remote_copy(
                    src_ref=block,
                    dst_ref=block,
                    send_sem=face_send.at[side, 2 + chip],
                    recv_sem=face_recv.at[side, g],
                    device_id=(gx, gy + 1 - 2 * core),
                    device_id_type=MESH,
                )
            )
            relays[-1].start()

    for copy in edges:
        copy.wait_recv()
    for f in range(5):
        ext[UP_Y[f], pl.ds(PITCH + 7, 8, stride=PITCH), :] = south[f]
        ext[DOWN_Y[f], pl.ds(PITCH + 24, 8, stride=PITCH), :] = north[f]
    order[pl.ds(2 * PITCH + 6, 8, stride=PITCH), :] = south[5]
    order[pl.ds(2 * PITCH + 7, 8, stride=PITCH), :] = south[6]
    order[pl.ds(2 * PITCH + 24, 8, stride=PITCH), :] = north[5]
    order[pl.ds(2 * PITCH + 25, 8, stride=PITCH), :] = north[6]

    for chip in range(2):
        for side, dst in enumerate((below, above)):
            g = 2 * chip + 1 - core
            block = face_block(dst, g)
            pltpu.make_async_copy(block, block, face_recv.at[side, g]).wait()

    for f in range(7):
        for dst in (below, above):
            for r in range(0, 24, 8):
                dst[f, pl.ds(64 + r, 8), :] = dst[f, pl.ds(r, 8), :]
    s = shift[0, 0]
    begin_low = lax.rem(gy * CY - 2 - s * plane_low + 128, 64)
    begin_high = lax.rem(gy * CY - 2 + s * plane_high + 128, 64)
    for src, begin, components, layer, layers in (
        (below, begin_low, UP_X, 0, (0, 1)),
        (above, begin_high, DOWN_X, 9, (10, 11)),
    ):
        for f, c in enumerate(components):
            for k in (0, 8, 10):
                ext[c, pl.ds(layer * PITCH + 7 + k, 8), :] = src[f, pl.ds(begin + 1 + k, 8), :]
        for f, l in zip((5, 6), layers):
            for k in (0, 8, 12):
                order[pl.ds(l * PITCH + 6 + k, 8), :] = src[f, pl.ds(begin + k, 8), :]

    collide(ext, order, potential, solid, dmap, wmap, out, new_order)
    @pl.loop(1, FAR)
    def _(k):
        arrived(far, far_recv, lax.rem(z + k, FAR))

    summed = total([far[h] for h in range(FAR)])
    mine = pltpu.roll(summed, lax.rem(NZ - 4 * z, NZ), 1)
    force[0:1, :] = mine[0:1, 0:4]
    force[1:2, :] = pltpu.roll(mine, NZ // 2, 1)[0:1, 0:4]
    force[2:3, :] = mine[1:2, 0:4]

    for copy in faces + edges + relays:
        copy.wait_send()

    for peer in peers:
        near_copy(peer).wait_send()

    @pl.loop(1, FAR)
    def _(k):
        far_copy(k).wait_send()


def write(pop, order, force, new_pop, new_order, new_force, sem):
    parts = [(0, 5), (5, 5), (10, 5), (15, 4)]
    copies = [
        pltpu.make_async_copy(pop.at[pl.ds(c, n)], new_pop.at[pl.ds(c, n)], sem.at[i])
        for i, (c, n) in enumerate(parts)
    ]
    copies.append(pltpu.make_async_copy(order, new_order, sem.at[4]))
    copies.append(pltpu.make_async_copy(force, new_force, sem.at[5]))
    for copy in copies:
        copy.start()
    for copy in copies:
        copy.wait()


VM = pl.BlockSpec(memory_space=pltpu.VMEM)
SM = pl.BlockSpec(memory_space=pltpu.SMEM)
HB = pl.BlockSpec(memory_space=pltpu.HBM)


def shaped(*dims, dtype=F32):
    return jax.ShapeDtypeStruct(dims, dtype)


def per_device(
    populations,
    order_field,
    solid_flags,
    plane_flags,
    shear_shift,
    link_site,
    link_dir,
    link_colloid,
    link_count,
    colloid_slot,
    colloid_speed,
):
    new_pop, new_order, force = pl.pallas_call(
        step,
        out_shape=(
            pltpu.VMEM((19, ROWS, NZ), F32),
            pltpu.VMEM((ROWS, NZ), F32),
            pltpu.VMEM((3, 4), F32),
        ),
        in_specs=[HB] * 11,
        out_specs=[VM] * 3,
        scratch_shapes=[
            pltpu.VMEM((ROWS, NZ), F32),
            pltpu.VMEM((ROWS, NZ), I32),
            pltpu.SMEM((128,), I32),
            pltpu.SMEM((1, 1), I32),
            pltpu.VMEM((8, NZ), I32),
            pltpu.VMEM((8, NZ), I32),
            pltpu.VMEM((8, NZ), I32),
            pltpu.SMEM((8,), I32),
            pltpu.VMEM((3, 2048), F32),
            pltpu.VMEM((16, NZ), I32),
            pltpu.VMEM((19, 10 * PITCH, NZ), F32),
            pltpu.VMEM((12 * PITCH, NZ), F32),
            pltpu.VMEM((10 * PITCH, NZ), F32),
            pltpu.VMEM((7, 88, NZ), F32),
            pltpu.VMEM((7, 88, NZ), F32),
            pltpu.VMEM((7, 8, NZ), F32),
            pltpu.VMEM((7, 8, NZ), F32),
            pltpu.VMEM((7, CY, NZ), F32),
            pltpu.VMEM((7, CY, NZ), F32),
            pltpu.VMEM((7, 8, NZ), F32),
            pltpu.VMEM((7, 8, NZ), F32),
            pltpu.VMEM((NEAR, 2, NZ), F32),
            pltpu.VMEM((NEAR, 2, NZ), F32),
            pltpu.VMEM((FAR, 2, NZ), F32),
            pltpu.VMEM((ROWS, NZ), I32),
            pltpu.VMEM((ROWS, NZ), F32),
            pltpu.VMEM((ROWS, NZ), F32),
            pltpu.SemaphoreType.DMA((CX + 10,)),
            pltpu.SemaphoreType.DMA((NEAR,)),
            pltpu.SemaphoreType.DMA((NEAR,)),
            pltpu.SemaphoreType.DMA((FAR,)),
            pltpu.SemaphoreType.DMA((FAR,)),
            pltpu.SemaphoreType.DMA((2, 4)),
            pltpu.SemaphoreType.DMA((2, 4)),
            pltpu.SemaphoreType.DMA((2,)),
            pltpu.SemaphoreType.DMA((2,)),
            pltpu.SemaphoreType.REGULAR,
        ],
        compiler_params=pltpu.CompilerParams(collective_id=0, has_side_effects=True),
        name="step",
    )(
        populations.reshape(19, ROWS, NZ),
        order_field.reshape(ROWS, NZ),
        solid_flags.reshape(ROWS, NZ),
        plane_flags,
        shear_shift.reshape(1, 1),
        link_site.reshape(8, NZ),
        link_dir.reshape(8, NZ),
        link_colloid.reshape(8, NZ),
        link_count,
        colloid_speed,
        colloid_slot.reshape(16, NZ),
    )
    new_pop, new_order, force = pl.pallas_call(
        write,
        out_shape=(shaped(19, ROWS, NZ), shaped(ROWS, NZ), shaped(3, 4)),
        in_specs=[VM] * 3,
        out_specs=[HB, HB, HB],
        scratch_shapes=[pltpu.SemaphoreType.DMA((6,))],
        name="write",
    )(*[pltpu.with_memory_space_constraint(v, pltpu.VMEM) for v in (new_pop, new_order, force)])
    return new_pop.reshape(populations.shape), new_order.reshape(order_field.shape), force


def solution(mesh):
    return jax.shard_map(
        per_device,
        mesh=mesh,
        in_specs=(
            P(None, "gx", "gy", None),
            P("gx", "gy", None),
            P("gx", "gy", None),
            P(),
            P(),
            P(("gx", "gy")),
            P(("gx", "gy")),
            P(("gx", "gy")),
            P(("gx", "gy")),
            P(),
            P(),
        ),
        out_specs=(P(None, "gx", "gy", None), P("gx", "gy", None), P(None, ("gx", "gy"))),
        check_vma=False,
    )
```
